512 devices in a mesh: ens: 32 (over z, y_hi, core), lon: 16 (over x, y_lo).
Axes of the slice: x: 4, y: 8 (y_hi: 2, y_lo: 4; y = y_hi * 4 + y_lo), z: 8, core: 2. Of those that a mesh axis runs over, the one named last changes fastest.
Arguments:
- fields: bfloat16 [32, 641, 4, 2048], P('ens', None, None, 'lon'), may hold values from -6 to 6
- observed: bfloat16 [72, 4, 2048], P(None, None, 'lon'), may hold values from -6 to 6
- conv_weight: float32 [641, 49], replicated, may hold values from -0.875 to 0.875
- norm_gain: float32 [641], replicated, may hold values from 0.1 to 1.9
- up_weight: bfloat16 [1282, 641], replicated, may hold values from -0.25 to 0.25
- down_weight: bfloat16 [641, 1282], replicated, may hold values from -0.15625 to 0.15625
- head_weight: bfloat16 [72, 641], replicated, may hold values from -0.25 to 0.25
Outputs:
- field_grad: bfloat16 [32, 641, 4, 2048], P('ens', None, None, 'lon')
- score_grad: float32 [32, 72, 4, 2048], P('ens', None, None, 'lon')
- conv_grad: float32 [641, 49], replicated
- gain_grad: float32 [641], replicated
The draws below stay inside these ranges and needn't reach their ends.
All inputs are finite; a program needn't handle non-finite values.
Results may differ from the reference program's by a relative error of at most 0.015.
Values may be sent and summed in bfloat16 or wider, within the bound.
No kernel may reach another device: no remote copies, remote signals or barrier semaphores. Data moves between devices by JAX's collectives and lax.ppermute only.
A program may use at most 64 MiB of HBM per device.

```python
import jax
import jax.numpy as jnp
from jax import lax

C = 641
FF = 1282
V = 72
ROWS = 4
LON = 2048
MEMBERS = 32


def block_levels(stream_key, dims, shards, smallest, largest):
    def one(axis_at, parts):
        draws = jax.random.uniform(jax.random.fold_in(jax.random.fold_in(stream_key, 6), axis_at), (parts,), jnp.float32, smallest / len(shards), largest / len(shards))
        return jnp.repeat(jnp.exp(draws), dims[axis_at] // parts).reshape((-1,) + (1,) * (len(dims) - axis_at - 1))

    factor_of = one(*shards[0])
    for cut in shards[1:]:
        factor_of = factor_of * one(*cut)
    return factor_of


def scatter_about(stream_key, dims, scale, bound, shards=(), kind=jnp.bfloat16):
    result = jax.random.normal(stream_key, dims, jnp.float32) * scale
    if len(shards) > 0:
        result = block_levels(stream_key, dims, shards, -0.22, 0.18) * result
    return jnp.clip(result, min=-bound, max=bound).astype(kind)


def setup_inputs(seed: int = 0) -> dict:
    key_of = jax.random.split(jax.random.key(seed), 8)
    return {
        "fields": scatter_about(key_of[0], (MEMBERS, C, ROWS, LON), 1.0, 6.0, ((0, 32), (3, 16))),
        "observed": scatter_about(key_of[1], (V, ROWS, LON), 1.0, 6.0, ((2, 16),)),
        "conv_weight": scatter_about(key_of[2], (C, 49), 49 ** -0.5, 0.875, (), jnp.float32),
        "norm_gain": jnp.clip(1.0 + 0.18 * jax.random.normal(key_of[3], (C,), jnp.float32), 0.1, 1.9),
        "up_weight": scatter_about(key_of[4], (FF, C), C ** -0.5, 0.25),
        "down_weight": scatter_about(key_of[5], (C, FF), FF ** -0.5, 0.15625),
        "head_weight": scatter_about(key_of[6], (V, C), C ** -0.5, 0.25),
    }


softening = 0.0625

def conv_taps(padded, conv_weight, nrows, ncols):
    summed = jnp.zeros((padded.shape[0], nrows, ncols), jnp.float32)
    for row_tap in range(7):
        for col_tap in range(7):
            summed = summed + conv_weight[:, row_tap * 7 + col_tap][:, None, None] * padded[:, row_tap:row_tap + nrows, col_tap:col_tap + ncols]
    return summed

def pointwise(conv_out, flat_field, norm_gain, up_weight, down_weight, head_weight):
    center = lax.optimization_barrier(jnp.mean(conv_out, 0))
    offset = conv_out - center
    spread = lax.optimization_barrier(jnp.mean(offset * offset, 0))
    normed = (offset * lax.rsqrt(spread + 1e-05) * norm_gain[:, None]).astype(jnp.bfloat16)
    pre_act = jnp.dot(up_weight, normed, preferred_element_type=jnp.float32)
    hidden = jax.nn.gelu(pre_act).astype(jnp.bfloat16)
    mixed_out = (flat_field.astype(jnp.float32) + jnp.dot(down_weight, hidden, preferred_element_type=jnp.float32)).astype(jnp.bfloat16)
    return jnp.dot(head_weight, mixed_out, preferred_element_type=jnp.float32).astype(jnp.bfloat16)

def pad_member(member):
    wrapped = jnp.concatenate([member[..., -3:], member, member[..., :3]], -1)
    return jnp.pad(wrapped, ((0, 0), (3, 3), (0, 0)))

def slope(delta):
    return delta * lax.rsqrt(delta * delta + softening)

def reference(fields, observed, conv_weight, norm_gain, up_weight, down_weight, head_weight):
    channels, nrows, ncols = (fields.shape[1], fields.shape[2], fields.shape[3])
    count = fields.shape[0]

    def local_fn(conv_out, flat_field, gain_in):
        return pointwise(conv_out, flat_field, gain_in, up_weight, down_weight, head_weight)

    def forward(member):
        padded = pad_member(member.astype(jnp.float32))
        conv_out = conv_taps(padded, conv_weight, nrows, ncols).reshape(channels, -1)
        return local_fn(conv_out, member.reshape(channels, -1), norm_gain)
    preds = lax.map(forward, fields)
    obs_flat = observed.reshape(observed.shape[0], -1).astype(jnp.float32)
    preds_float = preds.astype(jnp.float32)

    def score(own_pred):
        own_float = own_pred.astype(jnp.float32)
        pair_sum = lax.optimization_barrier(jnp.sum(slope(own_float[None] - preds_float), 0))
        return slope(own_float - obs_flat) - pair_sum / (count - 1)
    scores = lax.map(score, preds)

    def backward(items):
        member, grad_seed = items
        padded = pad_member(member.astype(jnp.float32))
        conv_out = conv_taps(padded, conv_weight, nrows, ncols).reshape(channels, -1)
        unused, pullback = jax.vjp(local_fn, conv_out, member.reshape(channels, -1), norm_gain)
        conv_cot, field_direct, gain_term = pullback(grad_seed.astype(jnp.bfloat16))
        cot_grid = conv_cot.reshape(channels, nrows, ncols)
        kernel_terms = []
        for row_tap in range(7):
            for col_tap in range(7):
                kernel_terms.append(lax.optimization_barrier(jnp.sum(cot_grid * padded[:, row_tap:row_tap + nrows, col_tap:col_tap + ncols], axis=(1, 2))))
        kernel_grad = jnp.stack(kernel_terms, 1)
        cot_pad = pad_member(cot_grid)
        adjoint = jnp.zeros((channels, nrows, ncols), jnp.float32)
        for row_tap in range(7):
            for col_tap in range(7):
                adjoint = adjoint + conv_weight[:, row_tap * 7 + col_tap][:, None, None] * cot_pad[:, 6 - row_tap:6 - row_tap + nrows, 6 - col_tap:6 - col_tap + ncols]
        field_out = (field_direct.astype(jnp.float32).reshape(channels, nrows, ncols) + adjoint).astype(jnp.bfloat16)
        return (field_out, kernel_grad, gain_term)
    field_grad, kernel_all, gain_all = lax.map(backward, (fields, scores))
    score_grad = scores.reshape(count, observed.shape[0], nrows, ncols)
    return (field_grad, score_grad, lax.optimization_barrier(jnp.sum(kernel_all, 0)), lax.optimization_barrier(jnp.sum(gain_all, 0)))
```

```python
import functools
import jax
import jax.numpy as jnp
from jax import lax
from jax.experimental import pallas as pl
from jax.experimental.pallas import tpu as pltpu
from jax.sharding import PartitionSpec as P

softening = 0.0625
GROUP = 16
F32, BF16 = jnp.float32, jnp.bfloat16
gelu_scale = 0.7978845608028654
gelu_cubic = 0.044715


def params(flags=None):
    return pltpu.CompilerParams(vmem_limit_bytes=60 * 1024 * 1024, flags=flags)


def whole(n):
    return [pl.BlockSpec(memory_space=pltpu.VMEM)] * n


def edge_place(row, lanes, before):
    line = lax.broadcasted_iota(jnp.int32, (16, lanes), 0) - 3 * row
    lane = lax.broadcasted_iota(jnp.int32, (16, lanes), 1)
    at = lane - (lanes - 3) if before else lane
    return ((line == at) & (at >= 0) & (at < 3)).astype(BF16)


def pack_edges(rows):
    lanes = rows[0].shape[1]
    out = []
    for before in (True, False):
        total = None
        for row, value in enumerate(rows):
            part = lax.dot_general(
                edge_place(row, lanes, before), value, (((1,), (1,)), ((), ())),
                preferred_element_type=F32,
            )
            total = part if total is None else total + part
        out.append(total.astype(BF16))
    return out


def unpack_edges(left, right, row, lanes):
    dims = (((0,), (0,)), ((), ()))
    return lax.dot_general(left, edge_place(row, lanes, True), dims, preferred_element_type=F32) + lax.dot_general(
        right, edge_place(row, lanes, False), dims, preferred_element_type=F32
    )


def shifted(x, edge, lane, s):
    n = x.shape[1]
    if s == 0:
        return x
    merged = jnp.where(lane < s, edge, x) if s > 0 else jnp.where(lane >= n + s, edge, x)
    return pltpu.roll(merged, (-s) % n, 1)


def pack_kernel(f_ref, fr_ref, right_ref, left_ref):
    channels, nrows, lanes = f_ref.shape
    full = channels // GROUP

    def body(g, _):
        start = pl.multiple_of(g * GROUP, GROUP)
        x = f_ref[pl.ds(start, GROUP)].astype(F32)
        for r in range(nrows):
            fr_ref[r, pl.ds(start, GROUP), :] = x[:, r, :].astype(BF16)
        return 0

    lax.fori_loop(0, full, body, 0)
    rest = channels - full * GROUP
    if rest:
        for r in range(nrows):
            fr_ref[r, full * GROUP :, :] = jnp.zeros((fr_ref.shape[1] - full * GROUP, lanes), BF16)
        x = f_ref[full * GROUP :].astype(F32)
        for r in range(nrows):
            fr_ref[r, full * GROUP : channels, :] = x[:, r, :].astype(BF16)
    right_ref[...], left_ref[...] = pack_edges([fr_ref[r] for r in range(nrows)])


def forward_kernel(
    channels, fr_ref, hl_ref, hr_ref, wg_ref, up_ref, down_ref, head_ref,
    pred_ref, xhat_ref, inv_ref, slope_ref, edge_ref, hidden_ref,
):
    nrows, padded, lanes = fr_ref.shape
    points = nrows * lanes
    for r in range(nrows):
        edge_ref[r] = unpack_edges(hl_ref[...], hr_ref[...], r, lanes)
    lane = lax.broadcasted_iota(jnp.int32, (GROUP, lanes), 1)

    def conv(g, sums):
        start = pl.multiple_of(g * GROUP, GROUP)
        at = pl.ds(start, GROUP)
        w = wg_ref[at, :]
        taps = {}
        acc = [jnp.zeros((GROUP, lanes), F32) for _ in range(nrows)]
        for b in range(7):
            xs = [
                shifted(fr_ref[r, at, :].astype(F32), edge_ref[r, at, :], lane, b - 3)
                for r in range(nrows)
            ]
            for a in range(7):
                t = a * 7 + b
                wt = jnp.broadcast_to(w[:, t : t + 1], (GROUP, lanes))
                for r_out in range(nrows):
                    r_in = r_out + a - 3
                    if 0 <= r_in < nrows:
                        acc[r_out] = acc[r_out] + wt * xs[r_in]
        for r in range(nrows):
            xhat_ref[r, at, :] = acc[r]
        return tuple(s + v for s, v in zip(sums, acc))

    zero = tuple(jnp.zeros((GROUP, lanes), F32) for _ in range(nrows))
    sums = lax.fori_loop(0, padded // GROUP, conv, zero)
    means = [jnp.sum(s, 0, keepdims=True) * (1.0 / channels) for s in sums]

    def spread(g, sums):
        at = pl.ds(pl.multiple_of(g * GROUP, GROUP), GROUP)
        live = lax.broadcasted_iota(jnp.int32, (GROUP, lanes), 0) + g * GROUP < channels
        out = []
        for r in range(nrows):
            offset = jnp.where(live, xhat_ref[r, at, :] - means[r], 0.0)
            xhat_ref[r, at, :] = offset
            out.append(sums[r] + offset * offset)
        return tuple(out)

    sums = lax.fori_loop(0, padded // GROUP, spread, zero)
    invs = [lax.rsqrt(jnp.sum(s, 0, keepdims=True) * (1.0 / channels) + 1e-05) for s in sums]
    for r in range(nrows):
        inv_ref[r] = invs[r]

    normed_rows = []
    gain = wg_ref[:, 49:50]
    for r in range(nrows):
        xh = xhat_ref[r] * invs[r]
        xhat_ref[r] = xh
        normed_rows.append((xh * gain).astype(BF16)[:channels])
    normed = jnp.concatenate(normed_rows, axis=1)
    hiddens = up_ref.shape[1]
    for start in range(0, hiddens, 256):
        stop = min(start + 256, hiddens)
        pre = lax.dot_general(
            up_ref[:, start:stop], normed, (((0,), (0,)), ((), ())), preferred_element_type=F32
        )
        square = pre * pre
        t = jnp.tanh(gelu_scale * (pre + gelu_cubic * (square * pre)))
        half = 0.5 * (1.0 + t)
        hidden_ref[start:stop, :] = (pre * half).astype(BF16)
        slope_ref[start:stop, :] = half + (0.5 * gelu_scale) * pre * (1.0 - t * t) * (
            1.0 + (3 * gelu_cubic) * square
        )
    lift = jnp.dot(down_ref[...], hidden_ref[...], preferred_element_type=F32)
    own = jnp.concatenate([fr_ref[r, :channels, :] for r in range(nrows)], axis=1)
    mixed = (own.astype(F32) + lift).astype(BF16)
    pred = jnp.dot(head_ref[...], mixed, preferred_element_type=F32).astype(BF16)
    pieces, deep, _ = pred_ref.shape
    per = pieces // nrows
    for p in range(pieces):
        r, i = p // per, p % per
        pred_ref[p] = pred[i * deep : (i + 1) * deep, r * lanes : (r + 1) * lanes]


def slope(delta):
    return delta * lax.rsqrt(delta * delta + softening)


def pair_kernel(p_ref, out_ref, x_ref):
    members, deep, lanes = p_ref.shape
    x_ref[...] = p_ref[...].astype(F32)

    def body(k, _):
        x = x_ref[:, k, :]
        total = jnp.zeros((members, lanes), F32)
        for j in range(members):
            total = total + slope(x - x[j : j + 1])
        out_ref[:, k, :] = total
        return 0

    lax.fori_loop(0, deep, body, 0)


def backward_kernel(
    channels, members, pred_ref, obs_ref, pair_ref, fr_ref, hl_ref, hr_ref, wg_ref, up_ref, down_ref, head_ref,
    xhat_ref, inv_ref, slope_ref,
    score_ref, cot_ref, direct_ref, out_ref, right_ref, left_ref, edge_ref, dpre_ref, grads_ref,
):
    nrows, padded, lanes = fr_ref.shape
    pieces, deep, _ = pred_ref.shape
    per = pieces // nrows
    for p in range(pieces):
        r, i = p // per, p % per
        rows, cols = slice(i * deep, (i + 1) * deep), slice(r * lanes, (r + 1) * lanes)
        delta = pred_ref[p].astype(F32) - obs_ref[rows, cols].astype(F32)
        score_ref[rows, cols] = slope(delta) - pair_ref[p] * (1.0 / (members - 1))
    score = score_ref[...]
    for r in range(nrows):
        edge_ref[r] = unpack_edges(hl_ref[...], hr_ref[...], r, lanes)
    down_dims = (((0,), (0,)), ((), ()))
    mixed_cot = lax.dot_general(
        head_ref[...], score.astype(BF16), down_dims, preferred_element_type=F32
    ).astype(BF16)
    for r in range(nrows):
        direct_ref[r, :channels, :] = mixed_cot[:, r * lanes : (r + 1) * lanes]
        direct_ref[r, channels:, :] = jnp.zeros((padded - channels, lanes), BF16)
    hiddens = up_ref.shape[1]
    for start in range(0, hiddens, 256):
        stop = min(start + 256, hiddens)
        hidden_cot = lax.dot_general(
            down_ref[:, start:stop], mixed_cot, down_dims, preferred_element_type=F32
        ).astype(BF16).astype(F32)
        dpre_ref[start:stop, :] = (hidden_cot * slope_ref[start:stop, :]).astype(BF16)
    normed_cot = jnp.dot(up_ref[...], dpre_ref[...], preferred_element_type=F32).astype(BF16)
    for r in range(nrows):
        cot_ref[r, :channels, :] = normed_cot[:, r * lanes : (r + 1) * lanes].astype(F32)
        cot_ref[r, channels:, :] = jnp.zeros((padded - channels, lanes), F32)

    gain = wg_ref[:, 49:50]
    gain_sum = None
    for r in range(nrows):
        nc = cot_ref[r]
        xh = xhat_ref[r]
        part = jnp.sum(nc * xh, 1, keepdims=True)
        gain_sum = part if gain_sum is None else gain_sum + part
        scaled = nc * gain
        m1 = jnp.sum(scaled, 0, keepdims=True) * (1.0 / channels)
        m2 = jnp.sum(scaled * xh, 0, keepdims=True) * (1.0 / channels)
        live = lax.broadcasted_iota(jnp.int32, (padded, lanes), 0) < channels
        cot_ref[r] = jnp.where(live, inv_ref[r] * (scaled - m1 - xh * m2), 0.0)
    right_ref[...], left_ref[...] = pack_edges([cot_ref[r].astype(BF16) for r in range(nrows)])
    lane = lax.broadcasted_iota(jnp.int32, (GROUP, lanes), 1)
    grads_ref[...] = jnp.where(lax.broadcasted_iota(jnp.int32, (padded, lanes), 1) == 49, gain_sum, 0.0)

    def taps(g, _):
        at = pl.ds(pl.multiple_of(g * GROUP, GROUP), GROUP)
        out = grads_ref[at, :]
        cots = [cot_ref[r, at, :] for r in range(nrows)]
        for b in range(7):
            xs = [
                shifted(fr_ref[r, at, :].astype(F32), edge_ref[r, at, :], lane, b - 3)
                for r in range(nrows)
            ]
            for a in range(7):
                acc = None
                for r_out in range(nrows):
                    r_in = r_out + a - 3
                    if 0 <= r_in < nrows:
                        part = cots[r_out] * xs[r_in]
                        acc = part if acc is None else acc + part
                out = jnp.where(lane == a * 7 + b, jnp.sum(acc, 1, keepdims=True), out)
        grads_ref[at, :] = out
        return 0

    lax.fori_loop(0, padded // GROUP, taps, 0)
    pieces, deep, wide = out_ref.shape
    flat = jnp.concatenate([grads_ref[...], jnp.zeros((wide - padded, lanes), F32)], 0).T
    for p in range(pieces):
        out_ref[p] = flat[p * deep : (p + 1) * deep]


def adjoint_kernel(cot_ref, hl_ref, hr_ref, wg_ref, direct_ref, out_ref, edge_ref):
    nrows, padded, lanes = cot_ref.shape
    for r in range(nrows):
        edge_ref[r] = unpack_edges(hl_ref[...], hr_ref[...], r, lanes)
    lane = lax.broadcasted_iota(jnp.int32, (GROUP, lanes), 1)

    def body(g, _):
        at = pl.ds(pl.multiple_of(g * GROUP, GROUP), GROUP)
        w = wg_ref[at, :]
        acc = [direct_ref[r, at, :].astype(F32) for r in range(nrows)]
        for b in range(7):
            xs = [shifted(cot_ref[r, at, :], edge_ref[r, at, :], lane, 3 - b) for r in range(nrows)]
            for a in range(7):
                t = a * 7 + b
                wt = jnp.broadcast_to(w[:, t : t + 1], (GROUP, lanes))
                for r_out in range(nrows):
                    r_in = r_out + a - 3
                    if 0 <= r_in < nrows:
                        acc[r_in] = acc[r_in] + wt * xs[r_out]
        for r in range(nrows):
            out_ref[r, at, :] = acc[r].astype(BF16)
        return 0

    lax.fori_loop(0, padded // GROUP, body, 0)


def call(kernel, name, outs, n_in, scratch=()):
    return pl.pallas_call(
        kernel,
        name=name,
        out_shape=[jax.ShapeDtypeStruct(s, d) for s, d in outs],
        in_specs=whole(n_in),
        out_specs=whole(len(outs)),
        scratch_shapes=list(scratch),
        compiler_params=params(),
    )


def pad_channels(channels):
    return -(-channels // GROUP) * GROUP


def pack(f):
    channels, nrows, lanes = f.shape
    padded = pad_channels(channels)
    return call(pack_kernel, "pack", [((nrows, padded, lanes), BF16), ((16, padded), BF16), ((16, padded), BF16)], 1)(f)


def forward(members, fr, hl, hr, wg, up, down, head):
    nrows, padded, lanes = fr.shape
    points = nrows * lanes
    channels, hiddens = down.shape
    return call(
        functools.partial(forward_kernel, channels), "forward",
        [((members, head.shape[0] * nrows // members, lanes), BF16), (fr.shape, F32), ((nrows, 1, lanes), F32), ((hiddens, points), F32)],
        7, [pltpu.VMEM(fr.shape, F32), pltpu.VMEM((hiddens, points), BF16)],
    )(fr, hl, hr, wg, up, down, head)


def backward(members, pieces, pred, obs, pair, fr, hl, hr, wg, up, down, head, xhat, inv, gslope):
    nrows, padded, lanes = fr.shape
    points = nrows * lanes
    channels, hiddens = down.shape
    return call(
        functools.partial(backward_kernel, channels, members), "backward",
        [(obs.shape, F32), (fr.shape, F32), (fr.shape, BF16), ((pieces, 64 // pieces, -(-padded // 128) * 128), F32), ((16, padded), BF16), ((16, padded), BF16)],
        13, [pltpu.VMEM(fr.shape, F32), pltpu.VMEM((hiddens, points), BF16), pltpu.VMEM((padded, lanes), F32)],
    )(pred, obs, pair, fr, hl, hr, wg, up, down, head, xhat, inv, gslope)


def pairs(p):
    return call(pair_kernel, "pairs", [(p.shape, F32)], 1, [pltpu.VMEM(p.shape, F32)])(p)[0]


def adjoint(cot, hl, hr, wg, direct):
    return call(adjoint_kernel, "adjoint", [(cot.shape, BF16)], 5, [pltpu.VMEM(cot.shape, F32)])(cot, hl, hr, wg, direct)[0]


def ring(axis):
    n = lax.axis_size(axis)
    up = [(i, (i + 1) % n) for i in range(n)]
    return up, [(j, i) for i, j in up]


def swap_edges(to_right, to_left):
    up, down = ring("lon")
    return lax.ppermute(to_right, "lon", up), lax.ppermute(to_left, "lon", down)


def shards(fields, observed, conv_weight, norm_gain, up_weight, down_weight, head_weight):
    _, channels, nrows, lanes = fields.shape
    nvars = observed.shape[0]
    members = lax.axis_size("ens")
    padded = pad_channels(channels)
    fr, to_right, to_left = pack(fields[0])
    hl, hr = swap_edges(to_right, to_left)
    wg = jnp.pad(jnp.concatenate([conv_weight, norm_gain[:, None]], 1), ((0, padded - channels), (0, 14)))
    pred, xhat, inv, gslope = forward(members, fr, hl, hr, wg, up_weight.T, down_weight, head_weight)
    pair = pairs(exchange(pred, "ens"))
    pair = exchange(pair, "ens")
    score, cot, direct, grads, to_right, to_left = backward(
        members, lax.axis_size("lon"), pred, observed.reshape(nvars, -1), pair, fr, hl, hr, wg, up_weight.T, down_weight, head_weight,
        xhat, inv, gslope,
    )
    cl, cr = swap_edges(to_right, to_left)
    field_out = adjoint(cot, cl, cr, wg, direct)[:, :channels].transpose(1, 0, 2)
    total = reduce_all(grads)
    return (field_out[None], score.reshape(1, nvars, nrows, lanes), total[:49, :channels].T, total[49, :channels])


def exchange(x, axis):
    return lax.all_to_all(x, axis, 0, 0, tiled=True)


def reduce_all(grads):
    pieces, deep, wide = grads.shape
    mine = jnp.sum(exchange(grads, "lon"), 0)
    mine = jnp.sum(exchange(jnp.broadcast_to(mine, (lax.axis_size("ens"), deep, wide)), "ens"), 0)
    total = exchange(jnp.broadcast_to(mine, (pieces, deep, wide)), "lon")
    return total.reshape(pieces * deep, wide)


def solution(mesh):
    in_specs = (P("ens", None, None, "lon"), P(None, None, "lon"), P(), P(), P(), P(), P())
    out_specs = (P("ens", None, None, "lon"), P("ens", None, None, "lon"), P(), P())
    return jax.shard_map(shards, mesh=mesh, in_specs=in_specs, out_specs=out_specs, check_vma=False)
```

```python
import functools
import jax
import jax.numpy as jnp
from jax import lax
from jax.experimental import pallas as pl
from jax.experimental.pallas import tpu as pltpu
from jax.sharding import PartitionSpec as P

softening = 0.0625
LANES, PAD, BLOCK = 128, 8, 32
F32, BF16 = jnp.float32, jnp.bfloat16
gelu_scale = 0.7978845608028654
gelu_cubic = 0.044715


def params(flags=None):
    return pltpu.CompilerParams(vmem_limit_bytes=60 * 1024 * 1024, flags=flags)


def whole(n):
    return [pl.BlockSpec(memory_space=pltpu.VMEM)] * n


def onehot(row_target, width):
    at = lax.broadcasted_iota(jnp.int32, (row_target.shape[0], width), 1)
    return (at == row_target).astype(BF16)


NN, NT, TN = (((1,), (0,)), ((), ())), (((1,), (1,)), ((), ())), (((0,), (0,)), ((), ()))


def mm(x, y, dims=NN):
    return lax.dot_general(x, y, dims, preferred_element_type=F32)


def cols(tile):
    return slice(tile * LANES, (tile + 1) * LANES)


def edges(blocks):
    fill = [jnp.zeros((16 - 3 * len(blocks), blocks[0].shape[1]), F32)]
    last = jnp.concatenate([x[-3:] for x in blocks] + fill, 0)
    first = jnp.concatenate([x[:3] for x in blocks] + fill, 0)
    return last.astype(BF16), first.astype(BF16)


def pack_kernel(f_ref, ft_ref, right_ref, left_ref, spread_ref):
    channels, nrows, lons = f_ref.shape
    tall = LANES * nrows
    target = lax.broadcasted_iota(jnp.int32, (tall, 1), 0)
    spread_ref[...] = onehot((target % LANES) * nrows + target // LANES, tall)
    eye = onehot(lax.broadcasted_iota(jnp.int32, (lons, 1), 0), lons)
    for tile in range(ft_ref.shape[2] // LANES):
        count = min(LANES, channels - tile * LANES)
        z = f_ref[tile * LANES : tile * LANES + count].reshape(count * nrows, lons)
        if count < LANES:
            z = jnp.concatenate([z.astype(F32), jnp.zeros((tall - count * nrows, lons), F32)], 0).astype(BF16)
        by_row = mm(spread_ref[...], z).astype(BF16)
        blocks = []
        for r in range(nrows):
            blocks.append(mm(eye, by_row[r * LANES : (r + 1) * LANES], NT))
            ft_ref[r, :, cols(tile)] = blocks[r].astype(BF16)
        right_ref[:, cols(tile)], left_ref[:, cols(tile)] = edges(blocks)


def fill_edges(x_ref, left, right):
    tiles, nrows, tall, _ = x_ref.shape
    lons = tall - 2 * PAD
    for tile in range(tiles):
        for r in range(nrows):
            x_ref[tile, r, PAD - 3 : PAD, :] = left[3 * r : 3 * r + 3, cols(tile)]
            x_ref[tile, r, PAD + lons : PAD + lons + 3, :] = right[3 * r : 3 * r + 3, cols(tile)]


def fill_fields(x_ref, ft_ref, hl_ref, hr_ref):
    tiles, nrows, tall, _ = x_ref.shape
    for tile in range(tiles):
        for r in range(nrows):
            x_ref[tile, r, PAD : tall - PAD, :] = ft_ref[r, :, cols(tile)].astype(F32)
    fill_edges(x_ref, hl_ref[...].astype(F32), hr_ref[...].astype(F32))


def conv_block(x_ref, wt_ref, tile, start, acc, flip):
    nrows = len(acc)
    tall = acc[0].shape[0]
    acc = [v.reshape(tall // 8, 8, LANES) for v in acc]
    for b in range(7):
        at = PAD + start + (3 - b if flip else b - 3)
        xs = [x_ref[tile, r, at : at + tall, :].reshape(tall // 8, 8, LANES) for r in range(nrows)]
        for a in range(7):
            w = wt_ref[tile, pl.ds(a * 7 + b, 8, stride=0), :][None]
            for r_out in range(nrows):
                r_in = r_out + a - 3
                if 0 <= r_in < nrows:
                    to, of = (r_in, r_out) if flip else (r_out, r_in)
                    acc[to] = acc[to] + w * xs[of]
    return [v.reshape(tall, LANES) for v in acc]


def forward_kernel(
    channels, ft_ref, hl_ref, hr_ref, wt_ref, up_ref, down_ref, head_ref,
    pred_ref, xhat_ref, inv_ref, pre_ref, x_ref, normed_ref, hidden_ref,
):
    nrows, lons, wide = ft_ref.shape
    tiles = wide // LANES
    fill_fields(x_ref, ft_ref, hl_ref, hr_ref)

    def conv(tile, _):
        for start in range(0, lons, BLOCK):
            acc = conv_block(x_ref, wt_ref, tile, start, [jnp.zeros((BLOCK, LANES), F32)] * nrows, False)
            for r in range(nrows):
                xhat_ref[tile, r, start : start + BLOCK, :] = acc[r]
        return 0

    lax.fori_loop(0, tiles, conv, 0)
    for r in range(nrows):
        total = xhat_ref[0, r]
        for tile in range(1, tiles):
            total = total + xhat_ref[tile, r]
        mean = jnp.sum(total, 1, keepdims=True) * (1.0 / channels)
        total = None
        for tile in range(tiles):
            offset = xhat_ref[tile, r] - mean
            xhat_ref[tile, r] = offset
            square = offset * offset
            live = channels - tile * LANES
            if live < LANES:
                square = jnp.where(lax.broadcasted_iota(jnp.int32, square.shape, 1) < live, square, 0.0)
            total = square if total is None else total + square
        inv = lax.rsqrt(jnp.sum(total, 1, keepdims=True) * (1.0 / channels) + 1e-05)
        inv_ref[r] = inv
        for tile in range(tiles):
            xhat = xhat_ref[tile, r] * inv
            xhat_ref[tile, r] = xhat
            gain = wt_ref[tile, 49:50, :]
            normed_ref[r * lons : (r + 1) * lons, cols(tile)] = (xhat * gain).astype(BF16)
    hiddens = up_ref.shape[1]
    normed = normed_ref[:, :channels]
    for start in range(0, hiddens, 256):
        stop = min(start + 256, hiddens)
        pre = mm(normed, up_ref[:, start:stop])
        pre_ref[:, start:stop] = pre
        t = jnp.tanh(pre * (gelu_scale + (gelu_scale * gelu_cubic) * (pre * pre)))
        hidden_ref[:, start:stop] = (pre * (0.5 + 0.5 * t)).astype(BF16)
    lift = mm(hidden_ref[...], down_ref[...], NT)
    own = jnp.concatenate([ft_ref[r, :, :channels] for r in range(nrows)], axis=0)
    mixed = (own.astype(F32) + lift).astype(BF16)
    pred = mm(head_ref[...], mixed, NT).astype(BF16)
    pieces, deep, _ = pred_ref.shape
    per = pieces // nrows
    for p in range(pieces):
        r, i = p // per, p % per
        pred_ref[p] = pred[i * deep : (i + 1) * deep, r * lons : (r + 1) * lons]


def slope_kernel(pre_ref, out_ref):
    def body(i, _):
        at = pl.ds(pl.multiple_of(i * 16, 16), 16)
        pre = pre_ref[at, :]
        square = pre * pre
        t = jnp.tanh(pre * (gelu_scale + (gelu_scale * gelu_cubic) * square))
        half = 0.5 + 0.5 * t
        out_ref[at, :] = half + pre * (1.0 - t * t) * (
            0.5 * gelu_scale + (1.5 * gelu_scale * gelu_cubic) * square
        )
        return 0

    lax.fori_loop(0, pre_ref.shape[0] // 16, body, 0)


def slope(delta):
    return delta * lax.rsqrt(delta * delta + softening)


def pair_kernel(p_ref, out_ref, x_ref):
    members, deep, lanes = p_ref.shape
    x_ref[...] = p_ref[...].astype(F32)

    def body(k, _):
        x = x_ref[:, k, :]
        total = jnp.zeros((members, lanes), F32)
        for j in range(members):
            total = total + slope(x - x[j : j + 1])
        out_ref[:, k, :] = total
        return 0

    lax.fori_loop(0, deep, body, 0)


def backward_kernel(
    channels, members, pred_ref, obs_ref, pair_ref, wt_ref, up_ref, down_ref, head_ref, xhat_ref, inv_ref, gs_ref,
    score_ref, cot_ref, direct_ref, gain_ref, right_ref, left_ref, dpre_ref,
):
    tiles, nrows, lons, _ = xhat_ref.shape
    points = nrows * lons
    pieces, deep, _ = pred_ref.shape
    per = pieces // nrows
    for p in range(pieces):
        r, i = p // per, p % per
        rows, at = slice(i * deep, (i + 1) * deep), slice(r * lons, (r + 1) * lons)
        delta = pred_ref[p].astype(F32) - obs_ref[rows, at].astype(F32)
        score_ref[rows, at] = slope(delta) - pair_ref[p] * (1.0 / (members - 1))
    mixed_cot = mm(score_ref[...].astype(BF16), head_ref[...], TN)
    rest = jnp.zeros((points, tiles * LANES - channels), F32)
    wide_cot = jnp.concatenate([mixed_cot, rest], 1).astype(BF16)
    for tile in range(tiles):
        direct_ref[tile] = wide_cot[:, cols(tile)]
    mixed_cot = mixed_cot.astype(BF16)
    hiddens = up_ref.shape[1]
    for start in range(0, hiddens, 256):
        stop = min(start + 256, hiddens)
        hidden_cot = mm(mixed_cot, down_ref[:, start:stop]).astype(BF16).astype(F32)
        dpre_ref[:, start:stop] = (hidden_cot * gs_ref[:, start:stop]).astype(BF16)
    normed_cot = mm(dpre_ref[...], up_ref[...], NT).astype(BF16).astype(F32)
    normed_cot = jnp.concatenate([normed_cot, rest], 1)
    gains = [None] * tiles
    for r in range(nrows):
        here = slice(r * lons, (r + 1) * lons)
        first = second = None
        for tile in range(tiles):
            nc = normed_cot[here, cols(tile)]
            xhat = xhat_ref[tile, r]
            product = nc * xhat
            part = jnp.sum(product, 0, keepdims=True)
            gains[tile] = part if r == 0 else gains[tile] + part
            gain = wt_ref[tile, 49:50, :]
            scaled = nc * gain
            crossed = product * gain
            cot_ref[tile, r] = scaled
            first = scaled if first is None else first + scaled
            second = crossed if second is None else second + crossed
        first = jnp.sum(first, 1, keepdims=True) * (1.0 / channels)
        second = jnp.sum(second, 1, keepdims=True) * (1.0 / channels)
        for tile in range(tiles):
            cot_ref[tile, r] = inv_ref[r] * (cot_ref[tile, r] - first - xhat_ref[tile, r] * second)
    for tile in range(tiles):
        gain_ref[tile] = gains[tile]
        right_ref[:, cols(tile)], left_ref[:, cols(tile)] = edges([cot_ref[tile, r] for r in range(nrows)])


def taps_kernel(ft_ref, hl_ref, hr_ref, cot_ref, gain_ref, out_ref, x_ref, sums_ref):
    nrows, lons, wide = ft_ref.shape
    tiles = wide // LANES
    fill_fields(x_ref, ft_ref, hl_ref, hr_ref)
    tall = 16

    def body(tile, _):
        for b in range(7):
            acc = [jnp.zeros((tall, LANES), F32)] * 7
            for start in range(0, lons, tall):
                at = PAD + start + b - 3
                xs = [x_ref[tile, r, at : at + tall, :] for r in range(nrows)]
                cs = [cot_ref[tile, r, start : start + tall, :] for r in range(nrows)]
                for a in range(7):
                    for r_out in range(nrows):
                        r_in = r_out + a - 3
                        if 0 <= r_in < nrows:
                            acc[a] = acc[a] + cs[r_out] * xs[r_in]
            for a in range(7):
                sums_ref[tile, a * 7 + b : a * 7 + b + 1, :] = jnp.sum(acc[a], 0, keepdims=True)
        sums_ref[tile, 49:50, :] = gain_ref[tile]
        return 0

    lax.fori_loop(0, tiles, body, 0)
    pieces, deep, _ = out_ref.shape
    for tile in range(tiles):
        for p in range(pieces):
            if p * deep < 50:
                live = min(deep, 50 - p * deep)
                out_ref[p, :live, cols(tile)] = sums_ref[tile, p * deep : p * deep + live, :]
                if live < deep:
                    out_ref[p, live:, cols(tile)] = jnp.zeros((deep - live, LANES), F32)
            else:
                out_ref[p, :, cols(tile)] = jnp.zeros((deep, LANES), F32)


def adjoint_kernel(cot_ref, hl_ref, hr_ref, wt_ref, direct_ref, out_ref, x_ref, gather_ref, row_ref):
    tiles, nrows, lons, _ = cot_ref.shape
    channels = out_ref.shape[0]
    tall = LANES * nrows
    for tile in range(tiles):
        for r in range(nrows):
            x_ref[tile, r, PAD : PAD + lons, :] = cot_ref[tile, r]
    fill_edges(x_ref, hl_ref[...].astype(F32), hr_ref[...].astype(F32))
    target = lax.broadcasted_iota(jnp.int32, (tall, 1), 0)
    gather_ref[...] = onehot((target % nrows) * LANES + target // nrows, tall)

    def one(tile, count):
        for start in range(0, lons, BLOCK):
            acc = [direct_ref[tile, r * lons + start : r * lons + start + BLOCK, :].astype(F32) for r in range(nrows)]
            acc = conv_block(x_ref, wt_ref, tile, start, acc, True)
            for r in range(nrows):
                row_ref[start : start + BLOCK, cols(r)] = acc[r].astype(BF16)
        flat = mm(gather_ref[: count * nrows], row_ref[...], NT).astype(BF16)
        return flat.reshape(count, nrows, lons)

    def body(tile, _):
        out_ref[pl.ds(pl.multiple_of(tile * LANES, LANES), LANES)] = one(tile, LANES)
        return 0

    full = channels // LANES
    lax.fori_loop(0, full, body, 0)
    if full < tiles:
        got = one(full, 4 * (-(-(channels - full * LANES) // 4)))
        out_ref[full * LANES :] = got[: channels - full * LANES]


def call(kernel, name, outs, n_in, scratch=(), flops=0, nbytes=0):
    return pl.pallas_call(
        kernel,
        name=name,
        out_shape=[jax.ShapeDtypeStruct(s, d) for s, d in outs],
        in_specs=whole(n_in),
        out_specs=whole(len(outs)),
        scratch_shapes=[pltpu.VMEM(s, d) for s, d in scratch],
        compiler_params=params(),
        cost_estimate=pl.CostEstimate(flops=flops, bytes_accessed=nbytes, transcendentals=0) if nbytes else None,
    )


def pack(f):
    channels, nrows, lons = f.shape
    wide = -(-channels // LANES) * LANES
    edge = ((16, wide), BF16)
    return call(
        pack_kernel, "pack", [((nrows, lons, wide), BF16), edge, edge], 1, [((LANES * nrows, LANES * nrows), BF16)]
    )(f)


def padded_shape(ft):
    nrows, lons, wide = ft.shape
    return wide // LANES, nrows, lons + 2 * PAD, LANES


def forward(members, ft, hl, hr, wt, up, down, head):
    nrows, lons, wide = ft.shape
    points = nrows * lons
    channels, hiddens = down.shape
    return call(
        functools.partial(forward_kernel, channels), "forward",
        [((members, head.shape[0] * nrows // members, lons), BF16), ((wide // LANES, nrows, lons, LANES), F32),
         ((nrows, lons, 1), F32), ((points, hiddens), F32)],
        7, [(padded_shape(ft), F32), ((points, wide), BF16), ((points, hiddens), BF16)],
    )(ft, hl, hr, wt, up, down, head)


def gelu_slope(pre):
    return call(slope_kernel, "slope", [(pre.shape, F32)], 1, (), 20 * pre.size, 8 * pre.size)(pre)[0]


def backward(members, pred, obs, pair, wt, up, down, head, xhat, inv, gslope):
    tiles, nrows, lons, _ = xhat.shape
    points, wide = nrows * lons, tiles * LANES
    channels, hiddens = down.shape
    edge = ((16, wide), BF16)
    return call(
        functools.partial(backward_kernel, channels, members), "backward",
        [(obs.shape, F32), (xhat.shape, F32), ((tiles, points, LANES), BF16), ((tiles, 1, LANES), F32), edge, edge],
        10, [((points, hiddens), BF16)],
    )(pred, obs, pair, wt, up, down, head, xhat, inv, gslope)


def taps(pieces, ft, hl, hr, cot, gains):
    wide = ft.shape[2]
    return call(
        taps_kernel, "taps", [((pieces, 64 // pieces, wide), F32)], 5,
        [(padded_shape(ft), F32), ((wide // LANES, 56, LANES), F32)], 224 * cot.size, 8 * cot.size,
    )(ft, hl, hr, cot, gains)[0]


def pairs(p):
    return call(pair_kernel, "pairs", [(p.shape, F32)], 1, [(p.shape, F32)])(p)[0]


def adjoint(channels, cot, hl, hr, wt, direct):
    tiles, nrows, lons, _ = cot.shape
    tall = LANES * nrows
    return call(
        adjoint_kernel, "adjoint", [((channels, nrows, lons), BF16)], 5,
        [((tiles, nrows, lons + 2 * PAD, LANES), F32), ((tall, tall), BF16), ((lons, tall), BF16)],
        224 * cot.size, 8 * cot.size,
    )(cot, hl, hr, wt, direct)[0]


def ring(axis):
    n = lax.axis_size(axis)
    up = [(i, (i + 1) % n) for i in range(n)]
    return up, [(j, i) for i, j in up]


def swap_edges(to_right, to_left):
    up, down = ring("lon")
    return lax.ppermute(to_right, "lon", up), lax.ppermute(to_left, "lon", down)


def shards(fields, observed, conv_weight, norm_gain, up_weight, down_weight, head_weight):
    _, channels, nrows, lons = fields.shape
    nvars = observed.shape[0]
    members, pieces = lax.axis_size("ens"), lax.axis_size("lon")
    up_weight = up_weight.T
    ft, to_right, to_left = pack(fields[0])
    hl, hr = swap_edges(to_right, to_left)
    tiles = ft.shape[2] // LANES
    wt = jnp.concatenate([conv_weight.T, norm_gain[None]], 0)
    wt = jnp.pad(wt, ((0, 6), (0, tiles * LANES - channels))).reshape(56, tiles, LANES).transpose(1, 0, 2)
    pred, xhat, inv, pre = forward(members, ft, hl, hr, wt, up_weight, down_weight, head_weight)
    met = exchange(pred, "ens")
    gslope = gelu_slope(pre)
    pair = exchange(pairs(met), "ens")
    score, cot, direct, gains, to_right, to_left = backward(
        members, pred, observed.reshape(nvars, -1), pair, wt, up_weight, down_weight, head_weight, xhat, inv, gslope
    )
    edges_in = swap_edges(to_right, to_left)
    field_out, total = reduce_beside(
        taps(pieces, ft, hl, hr, cot, gains), edges_in, lambda cl, cr: adjoint(channels, cot, cl, cr, wt, direct)
    )
    return (field_out[None], score.reshape(1, nvars, nrows, lons), total[:49, :channels].T, total[49, :channels])


def exchange(x, axis):
    return lax.all_to_all(x, axis, 0, 0, tiled=True)


def reduce_beside(grads, edges_in, work):
    pieces, deep, wide = grads.shape
    parts, edges_in = lax.optimization_barrier((exchange(grads, "lon"), edges_in))
    mine = jnp.sum(parts, 0).astype(BF16)
    parts = exchange(jnp.broadcast_to(mine, (lax.axis_size("ens"), deep, wide)), "ens")
    parts, done = lax.optimization_barrier((parts, work(*edges_in)))
    mine = jnp.sum(parts.astype(F32), 0)
    total = exchange(jnp.broadcast_to(mine, (pieces, deep, wide)), "lon")
    return done, total.reshape(pieces * deep, wide)


def solution(mesh):
    in_specs = (P("ens", None, None, "lon"), P(None, None, "lon"), P(), P(), P(), P(), P())
    out_specs = (P("ens", None, None, "lon"), P("ens", None, None, "lon"), P(), P())
    return jax.shard_map(shards, mesh=mesh, in_specs=in_specs, out_specs=out_specs, check_vma=False)
```

```python
import functools
import jax
import jax.numpy as jnp
from jax import lax
from jax.experimental import pallas as pl
from jax.experimental.pallas import tpu as pltpu
from jax.sharding import PartitionSpec as P

softening = 0.0625
LANES, PAD, BLOCK = 128, 8, 32
F32, BF16 = jnp.float32, jnp.bfloat16
gelu_scale = 0.7978845608028654
gelu_cubic = 0.044715


def params(flags=None):
    return pltpu.CompilerParams(vmem_limit_bytes=24 * 1024 * 1024, flags=flags)


def whole(n):
    return [pl.BlockSpec(memory_space=pltpu.VMEM)] * n


def onehot(row_target, width):
    at = lax.broadcasted_iota(jnp.int32, (row_target.shape[0], width), 1)
    return (at == row_target).astype(BF16)


NN, NT, TN = (((1,), (0,)), ((), ())), (((1,), (1,)), ((), ())), (((0,), (0,)), ((), ()))


def mm(x, y, dims=NN):
    return lax.dot_general(x, y, dims, preferred_element_type=F32)


def cols(tile):
    return slice(tile * LANES, (tile + 1) * LANES)


def edges(blocks):
    fill = [jnp.zeros((16 - 3 * len(blocks), blocks[0].shape[1]), F32)]
    last = jnp.concatenate([x[-3:] for x in blocks] + fill, 0)
    first = jnp.concatenate([x[:3] for x in blocks] + fill, 0)
    return last.astype(BF16), first.astype(BF16)


def pack_kernel(f_ref, ft_ref, right_ref, left_ref, flat_ref):
    channels, nrows, lons = f_ref.shape
    tall = LANES * nrows
    eye = onehot(lax.broadcasted_iota(jnp.int32, (lons, 1), 0), lons)
    for tile in range(ft_ref.shape[2] // LANES):
        count = min(LANES, channels - tile * LANES)
        z = f_ref[tile * LANES : tile * LANES + count].reshape(count * nrows, lons)
        if count < LANES:
            flat_ref[tile * tall :] = jnp.zeros((tall, lons), F32)
        flat_ref[tile * tall : tile * tall + count * nrows] = z.astype(F32)
        blocks = []
        for r in range(nrows):
            x = flat_ref[pl.ds(tile * tall + r, LANES, stride=nrows), :].astype(BF16)
            blocks.append(mm(eye, x, NT))
            ft_ref[r, :, cols(tile)] = blocks[r].astype(BF16)
        right_ref[:, cols(tile)], left_ref[:, cols(tile)] = edges(blocks)


def fill_edges(x_ref, left, right):
    tiles, nrows, tall, _ = x_ref.shape
    lons = tall - 2 * PAD
    for tile in range(tiles):
        for r in range(nrows):
            x_ref[tile, r, PAD - 3 : PAD, :] = left[3 * r : 3 * r + 3, cols(tile)]
            x_ref[tile, r, PAD + lons : PAD + lons + 3, :] = right[3 * r : 3 * r + 3, cols(tile)]


def fill_fields(x_ref, ft_ref, hl_ref, hr_ref):
    tiles, nrows, tall, _ = x_ref.shape
    for tile in range(tiles):
        for r in range(nrows):
            x_ref[tile, r, PAD : tall - PAD, :] = ft_ref[r, :, cols(tile)].astype(F32)
    fill_edges(x_ref, hl_ref[...].astype(F32), hr_ref[...].astype(F32))


def conv_block(x_ref, wt_ref, tile, start, acc, flip):
    nrows = len(acc)
    tall = acc[0].shape[0]
    acc = [v.reshape(tall // 8, 8, LANES) for v in acc]
    for b in range(7):
        at = PAD + start + (3 - b if flip else b - 3)
        xs = [x_ref[tile, r, at : at + tall, :].reshape(tall // 8, 8, LANES) for r in range(nrows)]
        for a in range(7):
            w = wt_ref[tile, pl.ds(a * 7 + b, 8, stride=0), :][None]
            for r_out in range(nrows):
                r_in = r_out + a - 3
                if 0 <= r_in < nrows:
                    to, of = (r_in, r_out) if flip else (r_out, r_in)
                    acc[to] = acc[to] + w * xs[of]
    return [v.reshape(tall, LANES) for v in acc]


def forward_kernel(
    channels, ft_ref, hl_ref, hr_ref, wt_ref, up_ref, down_ref, head_ref,
    pred_ref, xhat_ref, inv_ref, pre_ref, x_ref, normed_ref, hidden_ref,
):
    nrows, lons, wide = ft_ref.shape
    tiles = wide // LANES
    fill_fields(x_ref, ft_ref, hl_ref, hr_ref)

    def conv(tile, _):
        for start in range(0, lons, BLOCK):
            acc = conv_block(x_ref, wt_ref, tile, start, [jnp.zeros((BLOCK, LANES), F32)] * nrows, False)
            for r in range(nrows):
                xhat_ref[tile, r, start : start + BLOCK, :] = acc[r]
        return 0

    lax.fori_loop(0, tiles, conv, 0)
    for r in range(nrows):
        total = xhat_ref[0, r]
        for tile in range(1, tiles):
            total = total + xhat_ref[tile, r]
        mean = jnp.sum(total, 1, keepdims=True) * (1.0 / channels)
        total = None
        for tile in range(tiles):
            offset = xhat_ref[tile, r] - mean
            xhat_ref[tile, r] = offset
            square = offset * offset
            live = channels - tile * LANES
            if live < LANES:
                square = jnp.where(lax.broadcasted_iota(jnp.int32, square.shape, 1) < live, square, 0.0)
            total = square if total is None else total + square
        inv = lax.rsqrt(jnp.sum(total, 1, keepdims=True) * (1.0 / channels) + 1e-05)
        inv_ref[r] = inv
        for tile in range(tiles):
            xhat = xhat_ref[tile, r] * inv
            xhat_ref[tile, r] = xhat
            gain = wt_ref[tile, 49:50, :]
            normed_ref[r * lons : (r + 1) * lons, cols(tile)] = (xhat * gain).astype(BF16)
    hiddens = up_ref.shape[1]
    normed = normed_ref[:, :channels]
    for start in range(0, hiddens, 256):
        stop = min(start + 256, hiddens)
        pre = mm(normed, up_ref[:, start:stop])
        pre_ref[:, start:stop] = pre
        t = jnp.tanh(pre * (gelu_scale + (gelu_scale * gelu_cubic) * (pre * pre)))
        hidden_ref[:, start:stop] = (pre * (0.5 + 0.5 * t)).astype(BF16)
    lift = mm(hidden_ref[...], down_ref[...], NT)
    own = jnp.concatenate([ft_ref[r, :, :channels] for r in range(nrows)], axis=0)
    mixed = (own.astype(F32) + lift).astype(BF16)
    pred = mm(head_ref[...], mixed, NT).astype(BF16)
    pieces, deep, _ = pred_ref.shape
    per = pieces // nrows
    for p in range(pieces):
        r, i = p // per, p % per
        pred_ref[p] = pred[i * deep : (i + 1) * deep, r * lons : (r + 1) * lons]


def slope_kernel(pre_ref, out_ref):
    def body(i, _):
        at = pl.ds(pl.multiple_of(i * 16, 16), 16)
        pre = pre_ref[at, :]
        square = pre * pre
        t = jnp.tanh(pre * (gelu_scale + (gelu_scale * gelu_cubic) * square))
        half = 0.5 + 0.5 * t
        out_ref[at, :] = half + pre * (1.0 - t * t) * (
            0.5 * gelu_scale + (1.5 * gelu_scale * gelu_cubic) * square
        )
        return 0

    lax.fori_loop(0, pre_ref.shape[0] // 16, body, 0)


def slope(delta):
    return delta * lax.rsqrt(delta * delta + softening)


def pair_kernel(p_ref, out_ref, x_ref, twice_ref, slopes_ref):
    members, deep, lanes = p_ref.shape
    x_ref[...] = p_ref[...].astype(F32)

    def body(k, _):
        x = x_ref[:, k, :]
        twice_ref[:members] = x
        twice_ref[members:] = x
        total = jnp.zeros((members, lanes), F32)
        for d in range(1, members // 2 + 1):
            here = slope(x - twice_ref[members - d : 2 * members - d])
            total = total + here
            if 2 * d != members:
                slopes_ref[d % 2, :members] = here
                slopes_ref[d % 2, members:] = here
                total = total - slopes_ref[d % 2, d : d + members]
        out_ref[:, k, :] = total
        return 0

    lax.fori_loop(0, deep, body, 0)


def backward_kernel(
    channels, members, pred_ref, obs_ref, pair_ref, wt_ref, up_ref, down_ref, head_ref, xhat_ref, inv_ref, gs_ref,
    score_ref, cot_ref, direct_ref, gain_ref, right_ref, left_ref, dpre_ref,
):
    tiles, nrows, lons, _ = xhat_ref.shape
    points = nrows * lons
    pieces, deep, _ = pred_ref.shape
    per = pieces // nrows
    for p in range(pieces):
        r, i = p // per, p % per
        rows, at = slice(i * deep, (i + 1) * deep), slice(r * lons, (r + 1) * lons)
        delta = pred_ref[p].astype(F32) - obs_ref[rows, at].astype(F32)
        score_ref[rows, at] = slope(delta) - pair_ref[p] * (1.0 / (members - 1))
    mixed_cot = mm(score_ref[...].astype(BF16), head_ref[...], TN)
    rest = jnp.zeros((points, tiles * LANES - channels), F32)
    wide_cot = jnp.concatenate([mixed_cot, rest], 1).astype(BF16)
    for tile in range(tiles):
        direct_ref[tile] = wide_cot[:, cols(tile)]
    mixed_cot = mixed_cot.astype(BF16)
    hiddens = up_ref.shape[1]
    for start in range(0, hiddens, 256):
        stop = min(start + 256, hiddens)
        hidden_cot = mm(mixed_cot, down_ref[:, start:stop]).astype(BF16).astype(F32)
        dpre_ref[:, start:stop] = (hidden_cot * gs_ref[:, start:stop]).astype(BF16)
    normed_cot = mm(dpre_ref[...], up_ref[...], NT).astype(BF16).astype(F32)
    normed_cot = jnp.concatenate([normed_cot, rest], 1)
    gains = [None] * tiles
    for r in range(nrows):
        here = slice(r * lons, (r + 1) * lons)
        first = second = None
        for tile in range(tiles):
            nc = normed_cot[here, cols(tile)]
            xhat = xhat_ref[tile, r]
            product = nc * xhat
            part = jnp.sum(product, 0, keepdims=True)
            gains[tile] = part if r == 0 else gains[tile] + part
            gain = wt_ref[tile, 49:50, :]
            scaled = nc * gain
            crossed = product * gain
            cot_ref[tile, r] = scaled
            first = scaled if first is None else first + scaled
            second = crossed if second is None else second + crossed
        first = jnp.sum(first, 1, keepdims=True) * (1.0 / channels)
        second = jnp.sum(second, 1, keepdims=True) * (1.0 / channels)
        for tile in range(tiles):
            cot_ref[tile, r] = inv_ref[r] * (cot_ref[tile, r] - first - xhat_ref[tile, r] * second)
    for tile in range(tiles):
        gain_ref[tile] = gains[tile]
        right_ref[:, cols(tile)], left_ref[:, cols(tile)] = edges([cot_ref[tile, r] for r in range(nrows)])


def taps_kernel(ft_ref, hl_ref, hr_ref, cot_ref, gain_ref, out_ref, x_ref, sums_ref):
    nrows, lons, wide = ft_ref.shape
    tiles = wide // LANES
    fill_fields(x_ref, ft_ref, hl_ref, hr_ref)
    tall = 16

    def body(tile, _):
        for b in range(7):
            acc = [jnp.zeros((tall, LANES), F32)] * 7
            for start in range(0, lons, tall):
                at = PAD + start + b - 3
                xs = [x_ref[tile, r, at : at + tall, :] for r in range(nrows)]
                cs = [cot_ref[tile, r, start : start + tall, :] for r in range(nrows)]
                for a in range(7):
                    for r_out in range(nrows):
                        r_in = r_out + a - 3
                        if 0 <= r_in < nrows:
                            acc[a] = acc[a] + cs[r_out] * xs[r_in]
            for a in range(7):
                sums_ref[tile, a * 7 + b : a * 7 + b + 1, :] = jnp.sum(acc[a], 0, keepdims=True)
        sums_ref[tile, 49:50, :] = gain_ref[tile]
        return 0

    lax.fori_loop(0, tiles, body, 0)
    pieces, deep, _ = out_ref.shape
    for tile in range(tiles):
        for p in range(pieces):
            if p * deep < 50:
                live = min(deep, 50 - p * deep)
                out_ref[p, :live, cols(tile)] = sums_ref[tile, p * deep : p * deep + live, :]
                if live < deep:
                    out_ref[p, live:, cols(tile)] = jnp.zeros((deep - live, LANES), F32)
            else:
                out_ref[p, :, cols(tile)] = jnp.zeros((deep, LANES), F32)


def adjoint_kernel(cot_ref, hl_ref, hr_ref, wt_ref, direct_ref, out_ref, x_ref, gather_ref, row_ref):
    tiles, nrows, lons, _ = cot_ref.shape
    channels = out_ref.shape[0]
    tall = LANES * nrows
    for tile in range(tiles):
        for r in range(nrows):
            x_ref[tile, r, PAD : PAD + lons, :] = cot_ref[tile, r]
    fill_edges(x_ref, hl_ref[...].astype(F32), hr_ref[...].astype(F32))
    target = lax.broadcasted_iota(jnp.int32, (tall, 1), 0)
    gather_ref[...] = onehot((target % nrows) * LANES + target // nrows, tall)

    def one(tile, count):
        for start in range(0, lons, BLOCK):
            acc = [direct_ref[tile, r * lons + start : r * lons + start + BLOCK, :].astype(F32) for r in range(nrows)]
            acc = conv_block(x_ref, wt_ref, tile, start, acc, True)
            for r in range(nrows):
                row_ref[start : start + BLOCK, cols(r)] = acc[r].astype(BF16)
        flat = mm(gather_ref[: count * nrows], row_ref[...], NT).astype(BF16)
        return flat.reshape(count, nrows, lons)

    def body(tile, _):
        out_ref[pl.ds(pl.multiple_of(tile * LANES, LANES), LANES)] = one(tile, LANES)
        return 0

    full = channels // LANES
    lax.fori_loop(0, full, body, 0)
    if full < tiles:
        got = one(full, 4 * (-(-(channels - full * LANES) // 4)))
        out_ref[full * LANES :] = got[: channels - full * LANES]


def call(kernel, name, outs, n_in, scratch=(), flops=0, nbytes=0):
    return pl.pallas_call(
        kernel,
        name=name,
        out_shape=[jax.ShapeDtypeStruct(s, d) for s, d in outs],
        in_specs=whole(n_in),
        out_specs=whole(len(outs)),
        scratch_shapes=[pltpu.VMEM(s, d) for s, d in scratch],
        compiler_params=params(),
        cost_estimate=pl.CostEstimate(flops=flops, bytes_accessed=nbytes, transcendentals=0) if nbytes else None,
    )


def pack(f):
    channels, nrows, lons = f.shape
    wide = -(-channels // LANES) * LANES
    edge = ((16, wide), BF16)
    return call(
        pack_kernel, "pack", [((nrows, lons, wide), BF16), edge, edge], 1, [((nrows * wide, lons), F32)]
    )(f)


def padded_shape(ft):
    nrows, lons, wide = ft.shape
    return wide // LANES, nrows, lons + 2 * PAD, LANES


def forward(members, ft, hl, hr, wt, up, down, head):
    nrows, lons, wide = ft.shape
    points = nrows * lons
    channels, hiddens = down.shape
    return call(
        functools.partial(forward_kernel, channels), "forward",
        [((members, head.shape[0] * nrows // members, lons), BF16), ((wide // LANES, nrows, lons, LANES), F32),
         ((nrows, lons, 1), F32), ((points, hiddens), F32)],
        7, [(padded_shape(ft), F32), ((points, wide), BF16), ((points, hiddens), BF16)],
    )(ft, hl, hr, wt, up, down, head)


def gelu_slope(pre):
    return call(slope_kernel, "slope", [(pre.shape, F32)], 1, (), 20 * pre.size, 8 * pre.size)(pre)[0]


def backward(members, pred, obs, pair, wt, up, down, head, xhat, inv, gslope):
    tiles, nrows, lons, _ = xhat.shape
    points, wide = nrows * lons, tiles * LANES
    channels, hiddens = down.shape
    edge = ((16, wide), BF16)
    return call(
        functools.partial(backward_kernel, channels, members), "backward",
        [(obs.shape, F32), (xhat.shape, F32), ((tiles, points, LANES), BF16), ((tiles, 1, LANES), F32), edge, edge],
        10, [((points, hiddens), BF16)],
    )(pred, obs, pair, wt, up, down, head, xhat, inv, gslope)


def taps(pieces, ft, hl, hr, cot, gains):
    wide = ft.shape[2]
    return call(
        taps_kernel, "taps", [((pieces, 64 // pieces, wide), F32)], 5,
        [(padded_shape(ft), F32), ((wide // LANES, 56, LANES), F32)], 224 * cot.size, 8 * cot.size,
    )(ft, hl, hr, cot, gains)[0]


def pairs(p):
    members, _, lanes = p.shape
    return call(
        pair_kernel, "pairs", [(p.shape, F32)], 1,
        [(p.shape, F32), ((2 * members, lanes), F32), ((2, 2 * members, lanes), F32)],
    )(p)[0]


def adjoint(channels, cot, hl, hr, wt, direct):
    tiles, nrows, lons, _ = cot.shape
    tall = LANES * nrows
    return call(
        adjoint_kernel, "adjoint", [((channels, nrows, lons), BF16)], 5,
        [((tiles, nrows, lons + 2 * PAD, LANES), F32), ((tall, tall), BF16), ((lons, tall), BF16)],
        224 * cot.size, 8 * cot.size,
    )(cot, hl, hr, wt, direct)[0]


def ring(axis):
    n = lax.axis_size(axis)
    up = [(i, (i + 1) % n) for i in range(n)]
    return up, [(j, i) for i, j in up]


def swap_edges(to_right, to_left):
    up, down = ring("lon")
    return lax.ppermute(to_right, "lon", up), lax.ppermute(to_left, "lon", down)


def shards(fields, observed, conv_weight, norm_gain, up_weight, down_weight, head_weight):
    _, channels, nrows, lons = fields.shape
    nvars = observed.shape[0]
    members, pieces = lax.axis_size("ens"), lax.axis_size("lon")
    up_weight = up_weight.T
    ft, to_right, to_left = pack(fields[0])
    hl, hr = swap_edges(to_right, to_left)
    tiles = ft.shape[2] // LANES
    wt = jnp.concatenate([conv_weight.T, norm_gain[None]], 0)
    wt = jnp.pad(wt, ((0, 6), (0, tiles * LANES - channels))).reshape(56, tiles, LANES).transpose(1, 0, 2)
    pred, xhat, inv, pre = forward(members, ft, hl, hr, wt, up_weight, down_weight, head_weight)
    met = exchange(pred, "ens")
    gslope = gelu_slope(pre)
    pair = exchange(pairs(met), "ens")
    score, cot, direct, gains, to_right, to_left = backward(
        members, pred, observed.reshape(nvars, -1), pair, wt, up_weight, down_weight, head_weight, xhat, inv, gslope
    )
    edges_in = swap_edges(to_right, to_left)
    field_out, total = reduce_beside(
        taps(pieces, ft, hl, hr, cot, gains), edges_in, lambda cl, cr: adjoint(channels, cot, cl, cr, wt, direct)
    )
    return (field_out[None], score.reshape(1, nvars, nrows, lons), total[:49, :channels].T, total[49, :channels])


def exchange(x, axis):
    return lax.all_to_all(x, axis, 0, 0, tiled=True)


def reduce_beside(grads, edges_in, work):
    pieces, deep, wide = grads.shape
    mine = jnp.sum(exchange(grads, "lon"), 0).astype(BF16)
    parts = exchange(jnp.broadcast_to(mine, (lax.axis_size("ens"), deep, wide)), "ens")
    parts, edges_in = lax.optimization_barrier((parts, edges_in))
    mine = jnp.sum(parts.astype(F32), 0)
    total = exchange(jnp.broadcast_to(mine, (pieces, deep, wide)), "lon")
    total, done = lax.optimization_barrier((total, work(*edges_in)))
    return done, total.reshape(pieces * deep, wide)


def solution(mesh):
    in_specs = (P("ens", None, None, "lon"), P(None, None, "lon"), P(), P(), P(), P(), P())
    out_specs = (P("ens", None, None, "lon"), P("ens", None, None, "lon"), P(), P())
    return jax.shard_map(shards, mesh=mesh, in_specs=in_specs, out_specs=out_specs, check_vma=False)
```

```python
import functools
import jax
import jax.numpy as jnp
from jax import lax
from jax.experimental import pallas as pl
from jax.experimental.pallas import tpu as pltpu
from jax.sharding import PartitionSpec as P

softening = 0.0625
LANES, PAD, BLOCK = 128, 8, 32
F32, BF16 = jnp.float32, jnp.bfloat16
gelu_scale = 0.7978845608028654
gelu_cubic = 0.044715


def params(flags=None):
    return pltpu.CompilerParams(vmem_limit_bytes=60 * 1024 * 1024, flags=flags)


def onehot(row_target, width):
    at = lax.broadcasted_iota(jnp.int32, (row_target.shape[0], width), 1)
    return (at == row_target).astype(BF16)


NN, NT, TN = (((1,), (0,)), ((), ())), (((1,), (1,)), ((), ())), (((0,), (0,)), ((), ()))


def mm(x, y, dims=NN):
    return lax.dot_general(x, y, dims, preferred_element_type=F32)


def cols(tile):
    return slice(tile * LANES, (tile + 1) * LANES)


def edges(blocks):
    fill = [jnp.zeros((16 - 3 * len(blocks), blocks[0].shape[1]), F32)]
    last = jnp.concatenate([x[-3:] for x in blocks] + fill, 0)
    first = jnp.concatenate([x[:3] for x in blocks] + fill, 0)
    return last.astype(BF16), first.astype(BF16)


def pack_kernel(f_hbm, ft_ref, right_ref, left_ref, flat_ref, f_ref, sems):
    channels, nrows, lons = f_ref.shape
    tall = LANES * nrows
    loads = []
    for tile in range(ft_ref.shape[2] // LANES):
        at = pl.ds(tile * LANES, min(LANES, channels - tile * LANES))
        loads.append(pltpu.make_async_copy(f_hbm.at[at], f_ref.at[at], sems.at[tile]))
        loads[tile].start()
    eye = onehot(lax.broadcasted_iota(jnp.int32, (lons, 1), 0), lons)
    for tile in range(ft_ref.shape[2] // LANES):
        count = min(LANES, channels - tile * LANES)
        loads[tile].wait()
        z = f_ref[tile * LANES : tile * LANES + count].reshape(count * nrows, lons)
        if count < LANES:
            flat_ref[tile * tall :] = jnp.zeros((tall, lons), F32)
        flat_ref[tile * tall : tile * tall + count * nrows] = z.astype(F32)
        blocks = []
        for r in range(nrows):
            x = flat_ref[pl.ds(tile * tall + r, LANES, stride=nrows), :].astype(BF16)
            blocks.append(mm(eye, x, NT))
            ft_ref[r, :, cols(tile)] = blocks[r].astype(BF16)
        right_ref[:, cols(tile)], left_ref[:, cols(tile)] = edges(blocks)


def fill_edges(x_ref, left, right):
    tiles, nrows, tall, _ = x_ref.shape
    lons = tall - 2 * PAD
    for tile in range(tiles):
        for r in range(nrows):
            x_ref[tile, r, PAD - 3 : PAD, :] = left[3 * r : 3 * r + 3, cols(tile)]
            x_ref[tile, r, PAD + lons : PAD + lons + 3, :] = right[3 * r : 3 * r + 3, cols(tile)]


def fill_fields(x_ref, ft_ref, hl_ref, hr_ref):
    tiles, nrows, tall, _ = x_ref.shape
    for tile in range(tiles):
        for r in range(nrows):
            x_ref[tile, r, PAD : tall - PAD, :] = ft_ref[r, :, cols(tile)].astype(F32)
    fill_edges(x_ref, hl_ref[...].astype(F32), hr_ref[...].astype(F32))


def start_all(pairs_of_refs, sems, first):
    copies = [pltpu.make_async_copy(a, b, sems.at[first + i]) for i, (a, b) in enumerate(pairs_of_refs)]
    for copy in copies:
        copy.start()
    return copies


def wait_all(copies):
    for copy in copies:
        copy.wait()


def conv_block(x_ref, wt_ref, tile, start, acc, flip):
    nrows = len(acc)
    tall = acc[0].shape[0]
    acc = [v.reshape(tall // 8, 8, LANES) for v in acc]
    for b in range(7):
        at = PAD + start + (3 - b if flip else b - 3)
        xs = [x_ref[tile, r, at : at + tall, :].reshape(tall // 8, 8, LANES) for r in range(nrows)]
        for a in range(7):
            w = wt_ref[tile, pl.ds(a * 7 + b, 8, stride=0), :][None]
            for r_out in range(nrows):
                r_in = r_out + a - 3
                if 0 <= r_in < nrows:
                    to, of = (r_in, r_out) if flip else (r_out, r_in)
                    acc[to] = acc[to] + w * xs[of]
    return [v.reshape(tall, LANES) for v in acc]


def forward_kernel(
    channels, ft_hbm, hl_ref, hr_ref, wt_ref, up_hbm, down_hbm, head_hbm,
    pred_ref, xhat_hbm, inv_hbm, pre_hbm,
    x_ref, normed_ref, hidden_ref, xhat_ref, inv_ref, pre_ref, up_ref, down_ref, head_ref, ft_ref, sems,
):
    fields = start_all([(ft_hbm, ft_ref)], sems, 6)
    loads = start_all([(up_hbm, up_ref), (down_hbm, down_ref), (head_hbm, head_ref)], sems, 0)
    nrows, lons, wide = ft_ref.shape
    tiles = wide // LANES
    wait_all(fields)
    fill_fields(x_ref, ft_ref, hl_ref, hr_ref)

    def conv(tile, _):
        for start in range(0, lons, BLOCK):
            acc = conv_block(x_ref, wt_ref, tile, start, [jnp.zeros((BLOCK, LANES), F32)] * nrows, False)
            for r in range(nrows):
                xhat_ref[tile, r, start : start + BLOCK, :] = acc[r]
        return 0

    lax.fori_loop(0, tiles, conv, 0)
    for r in range(nrows):
        total = xhat_ref[0, r]
        for tile in range(1, tiles):
            total = total + xhat_ref[tile, r]
        mean = jnp.sum(total, 1, keepdims=True) * (1.0 / channels)
        total = None
        for tile in range(tiles):
            offset = xhat_ref[tile, r] - mean
            xhat_ref[tile, r] = offset
            square = offset * offset
            live = channels - tile * LANES
            if live < LANES:
                square = jnp.where(lax.broadcasted_iota(jnp.int32, square.shape, 1) < live, square, 0.0)
            total = square if total is None else total + square
        inv = lax.rsqrt(jnp.sum(total, 1, keepdims=True) * (1.0 / channels) + 1e-05)
        inv_ref[r] = inv
        for tile in range(tiles):
            xhat = xhat_ref[tile, r] * inv
            xhat_ref[tile, r] = xhat
            gain = wt_ref[tile, 49:50, :]
            normed_ref[r * lons : (r + 1) * lons, cols(tile)] = (xhat * gain).astype(BF16)
    stores = start_all([(xhat_ref, xhat_hbm), (inv_ref, inv_hbm)], sems, 3)
    wait_all(loads)
    hiddens = up_ref.shape[1]
    normed = normed_ref[:, :channels]
    for start in range(0, hiddens, 256):
        stop = min(start + 256, hiddens)
        pre = mm(normed, up_ref[:, start:stop])
        pre_ref[:, start:stop] = pre
        t = jnp.tanh(pre * (gelu_scale + (gelu_scale * gelu_cubic) * (pre * pre)))
        hidden_ref[:, start:stop] = (pre * (0.5 + 0.5 * t)).astype(BF16)
    stores += start_all([(pre_ref, pre_hbm)], sems, 5)
    lift = mm(hidden_ref[...], down_ref[...], NT)
    own = jnp.concatenate([ft_ref[r, :, :channels] for r in range(nrows)], axis=0)
    mixed = (own.astype(F32) + lift).astype(BF16)
    pred = mm(head_ref[...], mixed, NT).astype(BF16)
    pieces, deep, _ = pred_ref.shape
    per = pieces // nrows
    for p in range(pieces):
        r, i = p // per, p % per
        pred_ref[p] = pred[i * deep : (i + 1) * deep, r * lons : (r + 1) * lons]
    wait_all(stores)


def slope_kernel(pre_ref, out_ref):
    def body(i, _):
        at = pl.ds(pl.multiple_of(i * 16, 16), 16)
        pre = pre_ref[at, :]
        square = pre * pre
        t = jnp.tanh(pre * (gelu_scale + (gelu_scale * gelu_cubic) * square))
        half = 0.5 + 0.5 * t
        out_ref[at, :] = half + pre * (1.0 - t * t) * (
            0.5 * gelu_scale + (1.5 * gelu_scale * gelu_cubic) * square
        )
        return 0

    lax.fori_loop(0, pre_ref.shape[0] // 16, body, 0)


def slope(delta):
    return delta * lax.rsqrt(delta * delta + softening)


def pair_kernel(p_ref, out_ref, x_ref, twice_ref, slopes_ref):
    members, deep, lanes = p_ref.shape
    x_ref[...] = p_ref[...].astype(F32)

    def body(k, _):
        x = x_ref[:, k, :]
        twice_ref[:members] = x
        twice_ref[members:] = x
        total = jnp.zeros((members, lanes), F32)
        for d in range(1, members // 2 + 1):
            here = slope(x - twice_ref[members - d : 2 * members - d])
            total = total + here
            if 2 * d != members:
                slopes_ref[d % 2, :members] = here
                slopes_ref[d % 2, members:] = here
                total = total - slopes_ref[d % 2, d : d + members]
        out_ref[:, k, :] = total
        return 0

    lax.fori_loop(0, deep, body, 0)


def backward_kernel(
    channels, members, pred_ref, obs_ref, pair_ref, hl_ref, hr_ref, wt_ref,
    up_hbm, down_hbm, head_hbm, xhat_hbm, inv_hbm, gs_hbm, ft_hbm,
    score_ref, cot_hbm, direct_hbm, right_ref, left_ref, out_ref,
    dpre_ref, cot_ref, direct_ref, sums_ref, x_ref,
    up_ref, down_ref, head_ref, xhat_ref, inv_ref, gs_ref, ft_ref, sems,
):
    first = start_all([(head_hbm, head_ref), (down_hbm, down_ref)], sems, 2)
    second = start_all([(gs_hbm, gs_ref)], sems, 4)
    third = start_all([(up_hbm, up_ref)], sems, 5)
    fourth = start_all([(xhat_hbm, xhat_ref), (inv_hbm, inv_ref), (ft_hbm, ft_ref)], sems, 6)
    tiles, nrows, lons, _ = xhat_ref.shape
    points = nrows * lons
    pieces, deep, _ = pred_ref.shape
    per = pieces // nrows
    for p in range(pieces):
        r, i = p // per, p % per
        rows, at = slice(i * deep, (i + 1) * deep), slice(r * lons, (r + 1) * lons)
        delta = pred_ref[p].astype(F32) - obs_ref[rows, at].astype(F32)
        score_ref[rows, at] = slope(delta) - pair_ref[p] * (1.0 / (members - 1))
    wait_all(first)
    mixed_cot = mm(score_ref[...].astype(BF16), head_ref[...], TN)
    rest = jnp.zeros((points, tiles * LANES - channels), F32)
    wide_cot = jnp.concatenate([mixed_cot, rest], 1).astype(BF16)
    for tile in range(tiles):
        direct_ref[tile] = wide_cot[:, cols(tile)]
    stores = start_all([(direct_ref, direct_hbm)], sems, 0)
    mixed_cot = mixed_cot.astype(BF16)
    hiddens = up_ref.shape[1]
    for start in range(0, hiddens, 256):
        stop = min(start + 256, hiddens)
        if start == 0:
            wait_all(second)
        hidden_cot = mm(mixed_cot, down_ref[:, start:stop]).astype(BF16).astype(F32)
        dpre_ref[:, start:stop] = (hidden_cot * gs_ref[:, start:stop]).astype(BF16)
    wait_all(third)
    normed_cot = mm(dpre_ref[...], up_ref[...], NT).astype(BF16).astype(F32)
    normed_cot = jnp.concatenate([normed_cot, rest], 1)
    wait_all(fourth)
    gains = [None] * tiles
    for r in range(nrows):
        here = slice(r * lons, (r + 1) * lons)
        first = second = None
        for tile in range(tiles):
            nc = normed_cot[here, cols(tile)]
            xhat = xhat_ref[tile, r]
            product = nc * xhat
            part = jnp.sum(product, 0, keepdims=True)
            gains[tile] = part if r == 0 else gains[tile] + part
            gain = wt_ref[tile, 49:50, :]
            scaled = nc * gain
            crossed = product * gain
            cot_ref[tile, r] = scaled
            first = scaled if first is None else first + scaled
            second = crossed if second is None else second + crossed
        first = jnp.sum(first, 1, keepdims=True) * (1.0 / channels)
        second = jnp.sum(second, 1, keepdims=True) * (1.0 / channels)
        for tile in range(tiles):
            cot_ref[tile, r] = inv_ref[r] * (cot_ref[tile, r] - first - xhat_ref[tile, r] * second)
    stores += start_all([(cot_ref, cot_hbm)], sems, 1)
    for tile in range(tiles):
        sums_ref[tile, 49:50, :] = gains[tile]
        right_ref[:, cols(tile)], left_ref[:, cols(tile)] = edges([cot_ref[tile, r] for r in range(nrows)])


    fill_fields(x_ref, ft_ref, hl_ref, hr_ref)
    add_taps(x_ref, cot_ref, sums_ref, out_ref)
    wait_all(stores)


def add_taps(x_ref, cot_ref, sums_ref, out_ref):
    tiles, nrows, lons, _ = cot_ref.shape
    tall = 16

    def body(tile, _):
        for b in range(7):
            acc = [jnp.zeros((tall, LANES), F32)] * 7
            for start in range(0, lons, tall):
                at = PAD + start + b - 3
                xs = [x_ref[tile, r, at : at + tall, :] for r in range(nrows)]
                cs = [cot_ref[tile, r, start : start + tall, :] for r in range(nrows)]
                for a in range(7):
                    for r_out in range(nrows):
                        r_in = r_out + a - 3
                        if 0 <= r_in < nrows:
                            acc[a] = acc[a] + cs[r_out] * xs[r_in]
            for a in range(7):
                sums_ref[tile, a * 7 + b : a * 7 + b + 1, :] = jnp.sum(acc[a], 0, keepdims=True)
        return 0

    lax.fori_loop(0, tiles, body, 0)
    pieces, deep, _ = out_ref.shape
    for tile in range(tiles):
        for p in range(pieces):
            if p * deep < 50:
                live = min(deep, 50 - p * deep)
                out_ref[p, :live, cols(tile)] = sums_ref[tile, p * deep : p * deep + live, :]
                if live < deep:
                    out_ref[p, live:, cols(tile)] = jnp.zeros((deep - live, LANES), F32)
            else:
                out_ref[p, :, cols(tile)] = jnp.zeros((deep, LANES), F32)


def adjoint_kernel(
    cot_hbm, hl_ref, hr_ref, wt_ref, direct_hbm, out_ref, x_ref, gather_ref, row_ref, direct_ref, sems
):
    tiles, nrows, lons, _ = cot_hbm.shape
    loads = start_all([(cot_hbm, x_ref.at[:, :, pl.ds(PAD, lons), :]), (direct_hbm, direct_ref)], sems, 0)
    channels = out_ref.shape[0]
    tall = LANES * nrows
    fill_edges(x_ref, hl_ref[...].astype(F32), hr_ref[...].astype(F32))
    target = lax.broadcasted_iota(jnp.int32, (tall, 1), 0)
    gather_ref[...] = onehot((target % nrows) * LANES + target // nrows, tall)
    wait_all(loads)

    def one(tile, count):
        for start in range(0, lons, BLOCK):
            acc = [direct_ref[tile, r * lons + start : r * lons + start + BLOCK, :].astype(F32) for r in range(nrows)]
            acc = conv_block(x_ref, wt_ref, tile, start, acc, True)
            for r in range(nrows):
                row_ref[start : start + BLOCK, cols(r)] = acc[r].astype(BF16)
        flat = mm(gather_ref[: count * nrows], row_ref[...], NT).astype(BF16)
        return flat.reshape(count, nrows, lons)

    def body(tile, _):
        out_ref[pl.ds(pl.multiple_of(tile * LANES, LANES), LANES)] = one(tile, LANES)
        return 0

    full = channels // LANES
    lax.fori_loop(0, full, body, 0)
    if full < tiles:
        got = one(full, 4 * (-(-(channels - full * LANES) // 4)))
        out_ref[full * LANES :] = got[: channels - full * LANES]


VM, HB = pltpu.VMEM, pltpu.HBM


def call(kernel, name, ins, outs, scratch=(), copies=0, flops=0, nbytes=0):
    sems = [pltpu.SemaphoreType.DMA((copies,))] if copies else []
    return pl.pallas_call(
        kernel,
        name=name,
        out_shape=[jax.ShapeDtypeStruct(s, d) for s, d, _ in outs],
        in_specs=[pl.BlockSpec(memory_space=m) for m in ins],
        out_specs=[pl.BlockSpec(memory_space=m) for _, _, m in outs],
        scratch_shapes=[pltpu.VMEM(s, d) for s, d in scratch] + sems,
        compiler_params=params(),
        cost_estimate=pl.CostEstimate(flops=flops, bytes_accessed=nbytes, transcendentals=0) if nbytes else None,
    )


def pack(f):
    channels, nrows, lons = f.shape
    wide = -(-channels // LANES) * LANES
    edge = ((16, wide), BF16, VM)
    return call(
        pack_kernel, "pack", [HB], [((nrows, lons, wide), BF16, VM), edge, edge],
        [((nrows * wide, lons), F32), (f.shape, BF16)], wide // LANES,
    )(f)


def padded_shape(ft):
    nrows, lons, wide = ft.shape
    return wide // LANES, nrows, lons + 2 * PAD, LANES


def forward(members, ft, hl, hr, wt, up, down, head):
    nrows, lons, wide = ft.shape
    points = nrows * lons
    channels, hiddens = down.shape
    xhat, inv, pre = ((wide // LANES, nrows, lons, LANES), F32), ((nrows, lons, 1), F32), ((points, hiddens), F32)
    return call(
        functools.partial(forward_kernel, channels), "forward", [HB] + [VM] * 3 + [HB] * 3,
        [((members, head.shape[0] * nrows // members, lons), BF16, VM), (*xhat, HB), (*inv, HB), (*pre, HB)],
        [(padded_shape(ft), F32), ((points, wide), BF16), ((points, hiddens), BF16), xhat, inv, pre,
         (up.shape, BF16), (down.shape, BF16), (head.shape, BF16), (ft.shape, BF16)], 7,
    )(ft, hl, hr, wt, up, down, head)


def gelu_slope(pre):
    points, hiddens = pre.shape
    tall = points // 8
    return pl.pallas_call(
        slope_kernel,
        name="slope",
        grid=(8,),
        out_shape=jax.ShapeDtypeStruct(pre.shape, F32),
        in_specs=[pl.BlockSpec((tall, hiddens), lambda i: (i, 0))],
        out_specs=pl.BlockSpec((tall, hiddens), lambda i: (i, 0)),
        compiler_params=params(),
        cost_estimate=pl.CostEstimate(flops=20 * pre.size, bytes_accessed=8 * pre.size, transcendentals=0),
    )(pre)


def backward(members, pieces, pred, obs, pair, hl, hr, wt, up, down, head, xhat, inv, gslope, ft):
    tiles, nrows, lons, _ = xhat.shape
    points, wide = nrows * lons, tiles * LANES
    channels, hiddens = down.shape
    edge = ((16, wide), BF16, VM)
    direct = ((tiles, points, LANES), BF16)
    far = (up, down, head, xhat, inv, gslope, ft)
    return call(
        functools.partial(backward_kernel, channels, members), "backward", [VM] * 6 + [HB] * 7,
        [(obs.shape, F32, VM), (xhat.shape, F32, HB), (*direct, HB), edge, edge, ((pieces, 64 // pieces, wide), F32, VM)],
        [((points, hiddens), BF16), (xhat.shape, F32), direct, ((tiles, 56, LANES), F32), (padded_shape(ft), F32)]
        + [(v.shape, v.dtype) for v in far],
        9, 224 * xhat.size, 8 * xhat.size,
    )(pred, obs, pair, hl, hr, wt, *far)


def pairs(p):
    members, _, lanes = p.shape
    return call(
        pair_kernel, "pairs", [VM], [(p.shape, F32, VM)],
        [(p.shape, F32), ((2 * members, lanes), F32), ((2, 2 * members, lanes), F32)],
    )(p)[0]


def adjoint(channels, cot, hl, hr, wt, direct):
    tiles, nrows, lons, _ = cot.shape
    tall = LANES * nrows
    return call(
        adjoint_kernel, "adjoint", [HB, VM, VM, VM, HB], [((channels, nrows, lons), BF16, VM)],
        [((tiles, nrows, lons + 2 * PAD, LANES), F32), ((tall, tall), BF16), ((lons, tall), BF16), (direct.shape, BF16)],
        2, 224 * cot.size, 8 * cot.size,
    )(cot, hl, hr, wt, direct)[0]


def ring(axis):
    n = lax.axis_size(axis)
    up = [(i, (i + 1) % n) for i in range(n)]
    return up, [(j, i) for i, j in up]


def swap_edges(to_right, to_left):
    up, down = ring("lon")
    return lax.ppermute(to_right, "lon", up), lax.ppermute(to_left, "lon", down)


def shards(fields, observed, conv_weight, norm_gain, up_weight, down_weight, head_weight):
    _, channels, nrows, lons = fields.shape
    nvars = observed.shape[0]
    members, pieces = lax.axis_size("ens"), lax.axis_size("lon")
    up_weight = up_weight.T
    ft, to_right, to_left = pack(fields[0])
    hl, hr = swap_edges(to_right, to_left)
    tiles = ft.shape[2] // LANES
    wt = jnp.concatenate([conv_weight.T, norm_gain[None]], 0)
    wt = jnp.pad(wt, ((0, 6), (0, tiles * LANES - channels))).reshape(56, tiles, LANES).transpose(1, 0, 2)
    pred, xhat, inv, pre = forward(members, ft, hl, hr, wt, up_weight, down_weight, head_weight)
    met = exchange(pred, "ens")
    pair = exchange(pairs(met), "ens")
    gslope = gelu_slope(pre)
    score, cot, direct, to_right, to_left, grads = backward(
        members, pieces, pred, observed.reshape(nvars, -1), pair, hl, hr, wt,
        up_weight, down_weight, head_weight, xhat, inv, gslope, ft,
    )
    edges_in = swap_edges(to_right, to_left)
    field_out, total = reduce_beside(grads, edges_in, lambda cl, cr: adjoint(channels, cot, cl, cr, wt, direct))
    return (field_out[None], score.reshape(1, nvars, nrows, lons), total[:49, :channels].T, total[49, :channels])


def exchange(x, axis):
    return lax.all_to_all(x, axis, 0, 0, tiled=True)


def reduce_beside(grads, edges_in, work):
    pieces, deep, wide = grads.shape
    mine = jnp.sum(exchange(grads, "lon"), 0).astype(BF16)
    parts = exchange(jnp.broadcast_to(mine, (lax.axis_size("ens"), deep, wide)), "ens")
    parts, edges_in = lax.optimization_barrier((parts, edges_in))
    mine = jnp.sum(parts.astype(F32), 0)
    total = exchange(jnp.broadcast_to(mine, (pieces, deep, wide)), "lon")
    total, done = lax.optimization_barrier((total, work(*edges_in)))
    return done, total.reshape(pieces * deep, wide)


def solution(mesh):
    in_specs = (P("ens", None, None, "lon"), P(None, None, "lon"), P(), P(), P(), P(), P())
    out_specs = (P("ens", None, None, "lon"), P("ens", None, None, "lon"), P(), P())
    return jax.shard_map(shards, mesh=mesh, in_specs=in_specs, out_specs=out_specs, check_vma=False)
```

```python
import functools
import jax
import jax.numpy as jnp
from jax import lax
from jax.experimental import pallas as pl
from jax.experimental.pallas import tpu as pltpu
from jax.sharding import PartitionSpec as P

softening = 0.0625
LANES, PAD, BLOCK = 128, 8, 32
F32, BF16 = jnp.float32, jnp.bfloat16
gelu_scale = 0.7978845608028654
gelu_cubic = 0.044715


def params(mib=60):
    return pltpu.CompilerParams(vmem_limit_bytes=mib * 1024 * 1024)


def onehot(row_target, width):
    at = lax.broadcasted_iota(jnp.int32, (row_target.shape[0], width), 1)
    return (at == row_target).astype(BF16)


NN, NT, TN = (((1,), (0,)), ((), ())), (((1,), (1,)), ((), ())), (((0,), (0,)), ((), ()))


def mm(x, y, dims=NN):
    return lax.dot_general(x, y, dims, preferred_element_type=F32)


def cols(tile):
    return slice(tile * LANES, (tile + 1) * LANES)


def edges(blocks):
    return jnp.concatenate([x[-3:] for x in blocks], 0), jnp.concatenate([x[:3] for x in blocks], 0)


def pack_kernel(f_hbm, ft_ref, right_ref, left_ref, flat_ref, f_ref, sems):
    channels, nrows, lons = f_ref.shape
    tall = LANES * nrows
    loads = []
    for tile in range(ft_ref.shape[2] // LANES):
        at = pl.ds(tile * LANES, min(LANES, channels - tile * LANES))
        loads.append(pltpu.make_async_copy(f_hbm.at[at], f_ref.at[at], sems.at[tile]))
        loads[tile].start()
    eye = onehot(lax.broadcasted_iota(jnp.int32, (lons, 1), 0), lons)
    for tile in range(ft_ref.shape[2] // LANES):
        count = min(LANES, channels - tile * LANES)
        loads[tile].wait()
        z = f_ref[tile * LANES : tile * LANES + count].reshape(count * nrows, lons)
        if count < LANES:
            flat_ref[tile * tall :] = jnp.zeros((tall, lons), F32)
        flat_ref[tile * tall : tile * tall + count * nrows] = z.astype(F32)
        blocks = []
        for r in range(nrows):
            x = flat_ref[pl.ds(tile * tall + r, LANES, stride=nrows), :].astype(BF16)
            blocks.append(mm(eye, x, NT))
            ft_ref[r, :, cols(tile)] = blocks[r].astype(BF16)
        fill = jnp.zeros((16 - 3 * nrows, LANES), F32)
        last, first = edges(blocks)
        right_ref[:, cols(tile)] = jnp.concatenate([last, fill], 0).astype(BF16)
        left_ref[:, cols(tile)] = jnp.concatenate([first, fill], 0).astype(BF16)


def fill_edges(x_ref, left, right):
    tiles, nrows, tall, _ = x_ref.shape
    lons = tall - 2 * PAD
    for tile in range(tiles):
        for r in range(nrows):
            x_ref[tile, r, PAD - 3 : PAD, :] = left[3 * r : 3 * r + 3, cols(tile)]
            x_ref[tile, r, PAD + lons : PAD + lons + 3, :] = right[3 * r : 3 * r + 3, cols(tile)]


def fill_fields(x_ref, ft_ref, hl_ref, hr_ref):
    tiles, nrows, tall, _ = x_ref.shape
    for tile in range(tiles):
        for r in range(nrows):
            x_ref[tile, r, PAD : tall - PAD, :] = ft_ref[r, :, cols(tile)].astype(F32)
    fill_edges(x_ref, hl_ref[...].astype(F32), hr_ref[...].astype(F32))


def start_all(pairs_of_refs, sems, first):
    copies = [pltpu.make_async_copy(a, b, sems.at[first + i]) for i, (a, b) in enumerate(pairs_of_refs)]
    for copy in copies:
        copy.start()
    return copies


def wait_all(copies):
    for copy in copies:
        copy.wait()


def conv_block(x_ref, wt_ref, tile, start, acc, flip):
    nrows = len(acc)
    tall = acc[0].shape[0]
    acc = [v.reshape(tall // 8, 8, LANES) for v in acc]
    for b in range(7):
        at = PAD + start + (3 - b if flip else b - 3)
        xs = [x_ref[tile, r, at : at + tall, :].reshape(tall // 8, 8, LANES) for r in range(nrows)]
        for a in range(7):
            w = wt_ref[tile, pl.ds(a * 7 + b, 8, stride=0), :][None]
            for r_out in range(nrows):
                r_in = r_out + a - 3
                if 0 <= r_in < nrows:
                    to, of = (r_in, r_out) if flip else (r_out, r_in)
                    acc[to] = acc[to] + w * xs[of]
    return [v.reshape(tall, LANES) for v in acc]


def forward_kernel(
    channels, ft_hbm, hl_ref, hr_ref, wt_ref, up_hbm, down_hbm, head_hbm,
    pred_ref, xhat_hbm, inv_hbm, pre_hbm,
    x_ref, normed_ref, hidden_ref, xhat_ref, inv_ref, pre_ref, up_ref, down_ref, head_ref, ft_ref, sems,
):
    fields = start_all([(ft_hbm, ft_ref)], sems, 6)
    loads = start_all([(up_hbm, up_ref), (down_hbm, down_ref), (head_hbm, head_ref)], sems, 0)
    nrows, lons, wide = ft_ref.shape
    tiles = wide // LANES
    wait_all(fields)
    fill_fields(x_ref, ft_ref, hl_ref, hr_ref)

    def conv(tile, _):
        for start in range(0, lons, BLOCK):
            acc = conv_block(x_ref, wt_ref, tile, start, [jnp.zeros((BLOCK, LANES), F32)] * nrows, False)
            for r in range(nrows):
                xhat_ref[tile, r, start : start + BLOCK, :] = acc[r]
        return 0

    lax.fori_loop(0, tiles, conv, 0)
    for r in range(nrows):
        total = xhat_ref[0, r]
        for tile in range(1, tiles):
            total = total + xhat_ref[tile, r]
        mean = jnp.sum(total, 1, keepdims=True) * (1.0 / channels)
        total = None
        for tile in range(tiles):
            offset = xhat_ref[tile, r] - mean
            xhat_ref[tile, r] = offset
            square = offset * offset
            live = channels - tile * LANES
            if live < LANES:
                square = jnp.where(lax.broadcasted_iota(jnp.int32, square.shape, 1) < live, square, 0.0)
            total = square if total is None else total + square
        inv = lax.rsqrt(jnp.sum(total, 1, keepdims=True) * (1.0 / channels) + 1e-05)
        inv_ref[r] = inv
        for tile in range(tiles):
            xhat = xhat_ref[tile, r] * inv
            xhat_ref[tile, r] = xhat
            gain = wt_ref[tile, 49:50, :]
            normed_ref[r * lons : (r + 1) * lons, cols(tile)] = (xhat * gain).astype(BF16)
    stores = start_all([(xhat_ref, xhat_hbm), (inv_ref, inv_hbm)], sems, 3)
    wait_all(loads)
    hiddens = up_ref.shape[1]
    normed = normed_ref[:, :channels]
    for start in range(0, hiddens, 256):
        stop = min(start + 256, hiddens)
        pre = mm(normed, up_ref[:, start:stop])
        pre_ref[:, start:stop] = pre
        t = jnp.tanh(pre * (gelu_scale + (gelu_scale * gelu_cubic) * (pre * pre)))
        hidden_ref[:, start:stop] = (pre * (0.5 + 0.5 * t)).astype(BF16)
    stores += start_all([(pre_ref, pre_hbm)], sems, 5)
    lift = mm(hidden_ref[...], down_ref[...], NT)
    own = jnp.concatenate([ft_ref[r, :, :channels] for r in range(nrows)], axis=0)
    mixed = (own.astype(F32) + lift).astype(BF16)
    pred = mm(head_ref[...], mixed, NT).astype(BF16)
    pieces, deep, _ = pred_ref.shape
    per = pieces // nrows
    for p in range(pieces):
        r, i = p // per, p % per
        pred_ref[p] = pred[i * deep : (i + 1) * deep, r * lons : (r + 1) * lons]
    wait_all(stores)


def slope_kernel(pre_ref, out_ref):
    def body(i, _):
        at = pl.ds(pl.multiple_of(i * 16, 16), 16)
        pre = pre_ref[at, :]
        square = pre * pre
        t = jnp.tanh(pre * (gelu_scale + (gelu_scale * gelu_cubic) * square))
        half = 0.5 + 0.5 * t
        out_ref[at, :] = half + pre * (1.0 - t * t) * (
            0.5 * gelu_scale + (1.5 * gelu_scale * gelu_cubic) * square
        )
        return 0

    lax.fori_loop(0, pre_ref.shape[0] // 16, body, 0)


def slope(delta):
    return delta * lax.rsqrt(delta * delta + softening)


def pair_kernel(p_ref, out_ref, x_ref, twice_ref, slopes_ref):
    members, deep, lanes = p_ref.shape
    x_ref[...] = p_ref[...].astype(F32)

    def body(k, _):
        x = x_ref[:, k, :]
        twice_ref[:members] = x
        twice_ref[members:] = x
        total = jnp.zeros((members, lanes), F32)
        for d in range(1, members // 2 + 1):
            here = slope(x - twice_ref[members - d : 2 * members - d])
            total = total + here
            if 2 * d != members:
                slopes_ref[d % 2, :members] = here
                slopes_ref[d % 2, members:] = here
                total = total - slopes_ref[d % 2, d : d + members]
        out_ref[:, k, :] = total
        return 0

    lax.fori_loop(0, deep, body, 0)


def backward_kernel(
    channels, members, next_ref, pred_ref, obs_ref, pair_ref, hl_ref, hr_ref, wt_ref,
    up_hbm, down_hbm, head_hbm, xhat_hbm, inv_hbm, gs_hbm, ft_hbm,
    score_ref, cot_hbm, direct_hbm, out_ref,
    dpre_ref, cot_ref, direct_ref, sums_ref, x_ref,
    up_ref, down_ref, head_ref, xhat_ref, inv_ref, gs_ref, ft_ref, sems,
):
    first = start_all([(head_hbm, head_ref), (down_hbm, down_ref)], sems, 2)
    second = start_all([(gs_hbm, gs_ref)], sems, 4)
    third = start_all([(up_hbm, up_ref)], sems, 5)
    fourth = start_all([(xhat_hbm, xhat_ref), (inv_hbm, inv_ref), (ft_hbm, ft_ref)], sems, 6)
    tiles, nrows, lons, _ = xhat_ref.shape
    points = nrows * lons
    pieces, deep, _ = pred_ref.shape
    per = pieces // nrows
    for p in range(pieces):
        r, i = p // per, p % per
        rows, at = slice(i * deep, (i + 1) * deep), slice(r * lons, (r + 1) * lons)
        delta = pred_ref[p].astype(F32) - obs_ref[rows, at].astype(F32)
        score_ref[rows, at] = slope(delta) - pair_ref[p] * (1.0 / (members - 1))
    wait_all(first)
    mixed_cot = mm(score_ref[...].astype(BF16), head_ref[...], TN)
    rest = jnp.zeros((points, tiles * LANES - channels), F32)
    wide_cot = jnp.concatenate([mixed_cot, rest], 1).astype(BF16)
    for tile in range(tiles):
        direct_ref[tile] = wide_cot[:, cols(tile)]
    stores = start_all([(direct_ref, direct_hbm)], sems, 0)
    mixed_cot = mixed_cot.astype(BF16)
    hiddens = up_ref.shape[1]
    for start in range(0, hiddens, 256):
        stop = min(start + 256, hiddens)
        if start == 0:
            wait_all(second)
        hidden_cot = mm(mixed_cot, down_ref[:, start:stop]).astype(BF16).astype(F32)
        dpre_ref[:, start:stop] = (hidden_cot * gs_ref[:, start:stop]).astype(BF16)
    wait_all(third)
    normed_cot = mm(dpre_ref[...], up_ref[...], NT).astype(BF16).astype(F32)
    normed_cot = jnp.concatenate([normed_cot, rest], 1)
    wait_all(fourth)
    gains = [None] * tiles
    for r in range(nrows):
        here = slice(r * lons, (r + 1) * lons)
        first = second = None
        for tile in range(tiles):
            nc = normed_cot[here, cols(tile)]
            xhat = xhat_ref[tile, r]
            product = nc * xhat
            part = jnp.sum(product, 0, keepdims=True)
            gains[tile] = part if r == 0 else gains[tile] + part
            gain = wt_ref[tile, 49:50, :]
            scaled = nc * gain
            crossed = product * gain
            cot_ref[tile, r] = scaled
            first = scaled if first is None else first + scaled
            second = crossed if second is None else second + crossed
        first = jnp.sum(first, 1, keepdims=True) * (1.0 / channels)
        second = jnp.sum(second, 1, keepdims=True) * (1.0 / channels)
        for tile in range(tiles):
            cot_ref[tile, r] = inv_ref[r] * (cot_ref[tile, r] - first - xhat_ref[tile, r] * second)
    stores += start_all([(cot_ref, cot_hbm)], sems, 1)
    for tile in range(tiles):
        sums_ref[tile, 48:, :] = jnp.zeros((sums_ref.shape[1] - 48, LANES), F32)
        sums_ref[tile, 49:50, :] = gains[tile]


    fill_fields(x_ref, ft_ref, hl_ref, hr_ref)
    add_taps(x_ref, cot_ref, sums_ref)
    send(next_ref[0], cot_ref, sums_ref, out_ref)
    wait_all(stores)


def add_taps(x_ref, cot_ref, sums_ref):
    tiles, nrows, lons, _ = cot_ref.shape
    tall = 16

    def body(tile, _):
        for b in range(7):
            acc = [jnp.zeros((tall, LANES), F32)] * 7
            for start in range(0, lons, tall):
                at = PAD + start + b - 3
                xs = [x_ref[tile, r, at : at + tall, :] for r in range(nrows)]
                cs = [cot_ref[tile, r, start : start + tall, :] for r in range(nrows)]
                for a in range(7):
                    for r_out in range(nrows):
                        r_in = r_out + a - 3
                        if 0 <= r_in < nrows:
                            acc[a] = acc[a] + cs[r_out] * xs[r_in]
            for a in range(7):
                sums_ref[tile, a * 7 + b : a * 7 + b + 1, :] = jnp.sum(acc[a], 0, keepdims=True)
        return 0

    lax.fori_loop(0, tiles, body, 0)


def send(right, cot_ref, sums_ref, out_ref):
    tiles, nrows, _, _ = cot_ref.shape
    pieces, tall, _ = out_ref.shape
    deep = tall - 3 * nrows
    for tile in range(tiles):
        last, first = edges([cot_ref[tile, r] for r in range(nrows)])
        for p in range(pieces):
            edge = jnp.where(right == p, last, first)
            share = sums_ref[tile, p * deep : (p + 1) * deep, :]
            out_ref[p, :, cols(tile)] = jnp.concatenate([edge, share], 0).astype(BF16)


def adjoint_kernel(
    cot_hbm, hl_ref, hr_ref, wt_ref, direct_hbm, out_ref, x_ref, gather_ref, row_ref, direct_ref, sems
):
    tiles, nrows, lons, _ = cot_hbm.shape
    loads = start_all([(cot_hbm, x_ref.at[:, :, pl.ds(PAD, lons), :]), (direct_hbm, direct_ref)], sems, 0)
    channels = out_ref.shape[0]
    tall = LANES * nrows
    fill_edges(x_ref, hl_ref[...].astype(F32), hr_ref[...].astype(F32))
    target = lax.broadcasted_iota(jnp.int32, (tall, 1), 0)
    gather_ref[...] = onehot((target % nrows) * LANES + target // nrows, tall)
    wait_all(loads)

    def one(tile, count):
        for start in range(0, lons, BLOCK):
            acc = [direct_ref[tile, r * lons + start : r * lons + start + BLOCK, :].astype(F32) for r in range(nrows)]
            acc = conv_block(x_ref, wt_ref, tile, start, acc, True)
            for r in range(nrows):
                row_ref[start : start + BLOCK, cols(r)] = acc[r].astype(BF16)
        flat = mm(gather_ref[: count * nrows], row_ref[...], NT).astype(BF16)
        return flat.reshape(count, nrows, lons)

    def body(tile, _):
        out_ref[pl.ds(pl.multiple_of(tile * LANES, LANES), LANES)] = one(tile, LANES)
        return 0

    full = channels // LANES
    lax.fori_loop(0, full, body, 0)
    if full < tiles:
        got = one(full, 4 * (-(-(channels - full * LANES) // 4)))
        out_ref[full * LANES :] = got[: channels - full * LANES]


VM, HB = pltpu.VMEM, pltpu.HBM


def call(kernel, name, ins, outs, scratch=(), copies=0, flops=0, nbytes=0, mib=60):
    sems = [pltpu.SemaphoreType.DMA((copies,))] if copies else []
    return pl.pallas_call(
        kernel,
        name=name,
        out_shape=[jax.ShapeDtypeStruct(s, d) for s, d, _ in outs],
        in_specs=[pl.BlockSpec(memory_space=m) for m in ins],
        out_specs=[pl.BlockSpec(memory_space=m) for _, _, m in outs],
        scratch_shapes=[pltpu.VMEM(s, d) for s, d in scratch] + sems,
        compiler_params=params(mib),
        cost_estimate=pl.CostEstimate(flops=flops, bytes_accessed=nbytes, transcendentals=0) if nbytes else None,
    )


def pack(f):
    channels, nrows, lons = f.shape
    wide = -(-channels // LANES) * LANES
    edge = ((16, wide), BF16, VM)
    return call(
        pack_kernel, "pack", [HB], [((nrows, lons, wide), BF16, VM), edge, edge],
        [((nrows * wide, lons), F32), (f.shape, BF16)], wide // LANES, mib=16,
    )(f)


def padded_shape(ft):
    nrows, lons, wide = ft.shape
    return wide // LANES, nrows, lons + 2 * PAD, LANES


def forward(members, ft, hl, hr, wt, up, down, head):
    nrows, lons, wide = ft.shape
    points = nrows * lons
    channels, hiddens = down.shape
    xhat, inv, pre = ((wide // LANES, nrows, lons, LANES), F32), ((nrows, lons, 1), F32), ((points, hiddens), F32)
    return call(
        functools.partial(forward_kernel, channels), "forward", [HB] + [VM] * 3 + [HB] * 3,
        [((members, head.shape[0] * nrows // members, lons), BF16, VM), (*xhat, HB), (*inv, HB), (*pre, HB)],
        [(padded_shape(ft), F32), ((points, wide), BF16), ((points, hiddens), BF16), xhat, inv, pre,
         (up.shape, BF16), (down.shape, BF16), (head.shape, BF16), (ft.shape, BF16)], 7,
    )(ft, hl, hr, wt, up, down, head)


def gelu_slope(pre):
    points, hiddens = pre.shape
    tall = points // 8
    return pl.pallas_call(
        slope_kernel,
        name="slope",
        grid=(8,),
        out_shape=jax.ShapeDtypeStruct(pre.shape, F32),
        in_specs=[pl.BlockSpec((tall, hiddens), lambda i: (i, 0))],
        out_specs=pl.BlockSpec((tall, hiddens), lambda i: (i, 0)),
        compiler_params=params(),
        cost_estimate=pl.CostEstimate(flops=20 * pre.size, bytes_accessed=8 * pre.size, transcendentals=0),
    )(pre)


def backward(members, pieces, right, pred, obs, pair, hl, hr, wt, up, down, head, xhat, inv, gslope, ft):
    tiles, nrows, lons, _ = xhat.shape
    points, wide = nrows * lons, tiles * LANES
    channels, hiddens = down.shape
    sums = pieces * (4 if 4 * pieces >= 56 else 16)
    tall = 3 * nrows + sums // pieces
    direct = ((tiles, points, LANES), BF16)
    far = (up, down, head, xhat, inv, gslope, ft)
    return call(
        functools.partial(backward_kernel, channels, members), "backward", [pltpu.SMEM] + [VM] * 6 + [HB] * 7,
        [(obs.shape, F32, VM), (xhat.shape, F32, HB), (*direct, HB), ((pieces, tall, wide), BF16, VM)],
        [((points, hiddens), BF16), (xhat.shape, F32), direct, ((tiles, sums, LANES), F32), (padded_shape(ft), F32)]
        + [(v.shape, v.dtype) for v in far],
        9, 224 * xhat.size, 8 * xhat.size,
    )(right, pred, obs, pair, hl, hr, wt, *far)


def pairs(p):
    members, _, lanes = p.shape
    return call(
        pair_kernel, "pairs", [VM], [(p.shape, F32, VM)],
        [(p.shape, F32), ((2 * members, lanes), F32), ((2, 2 * members, lanes), F32)], mib=16,
    )(p)[0]


def adjoint(channels, cot, hl, hr, wt, direct):
    tiles, nrows, lons, _ = cot.shape
    tall = LANES * nrows
    return call(
        adjoint_kernel, "adjoint", [HB, VM, VM, VM, HB], [((channels, nrows, lons), BF16, VM)],
        [((tiles, nrows, lons + 2 * PAD, LANES), F32), ((tall, tall), BF16), ((lons, tall), BF16), (direct.shape, BF16)],
        2, 224 * cot.size, 8 * cot.size,
    )(cot, hl, hr, wt, direct)[0]


def ring(axis):
    n = lax.axis_size(axis)
    up = [(i, (i + 1) % n) for i in range(n)]
    return up, [(j, i) for i, j in up]


def swap_edges(to_right, to_left):
    up, down = ring("lon")
    return lax.ppermute(to_right, "lon", up), lax.ppermute(to_left, "lon", down)


def shards(fields, observed, conv_weight, norm_gain, up_weight, down_weight, head_weight):
    _, channels, nrows, lons = fields.shape
    nvars = observed.shape[0]
    members, pieces = lax.axis_size("ens"), lax.axis_size("lon")
    up_weight = up_weight.T
    ft, to_right, to_left = pack(fields[0])
    hl, hr = swap_edges(to_right, to_left)
    tiles = ft.shape[2] // LANES
    wt = jnp.concatenate([conv_weight.T, norm_gain[None]], 0)
    wt = jnp.pad(wt, ((0, 6), (0, tiles * LANES - channels))).reshape(56, tiles, LANES).transpose(1, 0, 2)
    pred, xhat, inv, pre = forward(members, ft, hl, hr, wt, up_weight, down_weight, head_weight)
    met = exchange(pred, "ens")
    pair = exchange(pairs(met), "ens")
    gslope = gelu_slope(pre)
    here = lax.axis_index("lon")
    before, after = (here + pieces - 1) % pieces, (here + 1) % pieces
    score, cot, direct, sent = backward(
        members, pieces, after[None], pred, observed.reshape(nvars, -1), pair, hl, hr, wt,
        up_weight, down_weight, head_weight, xhat, inv, gslope, ft,
    )
    met = exchange(sent, "lon")
    field_out, total = reduce_beside(
        jnp.sum(met[:, 3 * nrows :].astype(F32), 0).astype(BF16),
        lambda: adjoint(channels, cot, met[before], met[after], wt, direct),
    )
    return (field_out[None], score.reshape(1, nvars, nrows, lons), total[:49, :channels].T, total[49, :channels])


def exchange(x, axis):
    return lax.all_to_all(x, axis, 0, 0, tiled=True)


def reduce_beside(mine, work):
    deep, wide = mine.shape
    pieces = lax.axis_size("lon")
    parts = exchange(jnp.broadcast_to(mine, (lax.axis_size("ens"), deep, wide)), "ens")
    parts, done = lax.optimization_barrier((parts, work()))
    mine = jnp.sum(parts.astype(F32), 0)
    total = exchange(jnp.broadcast_to(mine, (pieces, deep, wide)), "lon")
    return done, total.reshape(pieces * deep, wide)


def solution(mesh):
    in_specs = (P("ens", None, None, "lon"), P(None, None, "lon"), P(), P(), P(), P(), P())
    out_specs = (P("ens", None, None, "lon"), P("ens", None, None, "lon"), P(), P())
    return jax.shard_map(shards, mesh=mesh, in_specs=in_specs, out_specs=out_specs, check_vma=False)
```

```python
import functools
import jax
import jax.numpy as jnp
from jax import lax
from jax.experimental import pallas as pl
from jax.experimental.pallas import tpu as pltpu
from jax.sharding import PartitionSpec as P

softening = 0.0625
LANES, PAD, BLOCK = 128, 8, 32
F32, BF16 = jnp.float32, jnp.bfloat16
gelu_scale = 0.7978845608028654
gelu_cubic = 0.044715


def params(mib=60):
    return pltpu.CompilerParams(vmem_limit_bytes=mib * 1024 * 1024)


def onehot(row_target, width):
    at = lax.broadcasted_iota(jnp.int32, (row_target.shape[0], width), 1)
    return (at == row_target).astype(BF16)


NN, NT, TN = (((1,), (0,)), ((), ())), (((1,), (1,)), ((), ())), (((0,), (0,)), ((), ()))


def mm(x, y, dims=NN):
    return lax.dot_general(x, y, dims, preferred_element_type=F32)


def cols(tile):
    return slice(tile * LANES, (tile + 1) * LANES)


def edges(blocks):
    return jnp.concatenate([x[-3:] for x in blocks], 0), jnp.concatenate([x[:3] for x in blocks], 0)


def pack_kernel(f_ref, ft_ref, right_ref, left_ref, flat_ref):
    channels, nrows, lons = f_ref.shape
    tall = LANES * nrows
    eye = onehot(lax.broadcasted_iota(jnp.int32, (lons, 1), 0), lons)
    for tile in range(ft_ref.shape[2] // LANES):
        count = min(LANES, channels - tile * LANES)
        z = f_ref[tile * LANES : tile * LANES + count].reshape(count * nrows, lons)
        if count < LANES:
            flat_ref[tile * tall :] = jnp.zeros((tall, lons), F32)
        flat_ref[tile * tall : tile * tall + count * nrows] = z.astype(F32)
        blocks = []
        for r in range(nrows):
            x = flat_ref[pl.ds(tile * tall + r, LANES, stride=nrows), :].astype(BF16)
            blocks.append(mm(eye, x, NT))
            ft_ref[r, :, cols(tile)] = blocks[r].astype(BF16)
        fill = jnp.zeros((16 - 3 * nrows, LANES), F32)
        last, first = edges(blocks)
        right_ref[:, cols(tile)] = jnp.concatenate([last, fill], 0).astype(BF16)
        left_ref[:, cols(tile)] = jnp.concatenate([first, fill], 0).astype(BF16)


def fill_edges(x_ref, left, right):
    tiles, nrows, tall, _ = x_ref.shape
    lons = tall - 2 * PAD
    for tile in range(tiles):
        for r in range(nrows):
            x_ref[tile, r, PAD - 3 : PAD, :] = left[3 * r : 3 * r + 3, cols(tile)]
            x_ref[tile, r, PAD + lons : PAD + lons + 3, :] = right[3 * r : 3 * r + 3, cols(tile)]


def fill_fields(x_ref, ft_ref, hl_ref, hr_ref):
    tiles, nrows, tall, _ = x_ref.shape
    for tile in range(tiles):
        for r in range(nrows):
            x_ref[tile, r, PAD : tall - PAD, :] = ft_ref[r, :, cols(tile)].astype(F32)
    fill_edges(x_ref, hl_ref[...].astype(F32), hr_ref[...].astype(F32))


def start_all(pairs_of_refs, sems, first):
    copies = [pltpu.make_async_copy(a, b, sems.at[first + i]) for i, (a, b) in enumerate(pairs_of_refs)]
    for copy in copies:
        copy.start()
    return copies


def wait_all(copies):
    for copy in copies:
        copy.wait()


def conv_block(x_ref, wt_ref, tile, start, acc, flip):
    nrows = len(acc)
    tall = acc[0].shape[0]
    acc = [v.reshape(tall // 8, 8, LANES) for v in acc]
    for b in range(7):
        at = PAD + start + (3 - b if flip else b - 3)
        xs = [x_ref[tile, r, at : at + tall, :].reshape(tall // 8, 8, LANES) for r in range(nrows)]
        for a in range(7):
            w = wt_ref[tile, pl.ds(a * 7 + b, 8, stride=0), :][None]
            for r_out in range(nrows):
                r_in = r_out + a - 3
                if 0 <= r_in < nrows:
                    to, of = (r_in, r_out) if flip else (r_out, r_in)
                    acc[to] = acc[to] + w * xs[of]
    return [v.reshape(tall, LANES) for v in acc]


def forward_kernel(
    channels, ft_hbm, hl_ref, hr_ref, wt_ref, up_hbm, down_hbm, head_hbm,
    pred_ref, xhat_hbm, inv_hbm, pre_hbm,
    x_ref, normed_ref, hidden_ref, xhat_ref, inv_ref, pre_ref, up_ref, down_ref, head_ref, ft_ref, sems,
):
    fields = start_all([(ft_hbm, ft_ref)], sems, 6)
    loads = start_all([(up_hbm, up_ref), (down_hbm, down_ref), (head_hbm, head_ref)], sems, 0)
    nrows, lons, wide = ft_ref.shape
    tiles = wide // LANES
    wait_all(fields)
    fill_fields(x_ref, ft_ref, hl_ref, hr_ref)

    def conv(tile, _):
        for start in range(0, lons, BLOCK):
            acc = conv_block(x_ref, wt_ref, tile, start, [jnp.zeros((BLOCK, LANES), F32)] * nrows, False)
            for r in range(nrows):
                xhat_ref[tile, r, start : start + BLOCK, :] = acc[r]
        return 0

    lax.fori_loop(0, tiles, conv, 0)
    for r in range(nrows):
        total = xhat_ref[0, r]
        for tile in range(1, tiles):
            total = total + xhat_ref[tile, r]
        mean = jnp.sum(total, 1, keepdims=True) * (1.0 / channels)
        total = None
        for tile in range(tiles):
            offset = xhat_ref[tile, r] - mean
            xhat_ref[tile, r] = offset
            square = offset * offset
            live = channels - tile * LANES
            if live < LANES:
                square = jnp.where(lax.broadcasted_iota(jnp.int32, square.shape, 1) < live, square, 0.0)
            total = square if total is None else total + square
        inv = lax.rsqrt(jnp.sum(total, 1, keepdims=True) * (1.0 / channels) + 1e-05)
        inv_ref[r] = inv
        for tile in range(tiles):
            xhat = xhat_ref[tile, r] * inv
            xhat_ref[tile, r] = xhat
            gain = wt_ref[tile, 49:50, :]
            normed_ref[r * lons : (r + 1) * lons, cols(tile)] = (xhat * gain).astype(BF16)
    stores = start_all([(xhat_ref, xhat_hbm), (inv_ref, inv_hbm)], sems, 3)
    wait_all(loads)
    hiddens = up_ref.shape[1]
    normed = normed_ref[:, :channels]
    for start in range(0, hiddens, 256):
        stop = min(start + 256, hiddens)
        pre = mm(normed, up_ref[:, start:stop])
        pre_ref[:, start:stop] = pre
        t = jnp.tanh(pre * (gelu_scale + (gelu_scale * gelu_cubic) * (pre * pre)))
        hidden_ref[:, start:stop] = (pre * (0.5 + 0.5 * t)).astype(BF16)
    stores += start_all([(pre_ref, pre_hbm)], sems, 5)
    lift = mm(hidden_ref[...], down_ref[...], NT)
    own = jnp.concatenate([ft_ref[r, :, :channels] for r in range(nrows)], axis=0)
    mixed = (own.astype(F32) + lift).astype(BF16)
    pred = mm(head_ref[...], mixed, NT).astype(BF16)
    pieces, deep, _ = pred_ref.shape
    per = pieces // nrows
    for p in range(pieces):
        r, i = p // per, p % per
        pred_ref[p] = pred[i * deep : (i + 1) * deep, r * lons : (r + 1) * lons]
    wait_all(stores)


def slope_kernel(pre_ref, out_ref):
    def body(i, _):
        at = pl.ds(pl.multiple_of(i * 16, 16), 16)
        pre = pre_ref[at, :]
        square = pre * pre
        t = jnp.tanh(pre * (gelu_scale + (gelu_scale * gelu_cubic) * square))
        half = 0.5 + 0.5 * t
        bend = 0.5 * gelu_scale + (1.5 * gelu_scale * gelu_cubic) * square
        out_ref[at, :] = (half + pre * (1.0 - t * t) * bend).astype(BF16)
        return 0

    lax.fori_loop(0, pre_ref.shape[0] // 16, body, 0)


def slope(delta):
    return delta * lax.rsqrt(delta * delta + softening)


def pair_kernel(p_ref, out_ref, x_ref, twice_ref, slopes_ref, sum_ref):
    members, deep, lanes = p_ref.shape
    x_ref[...] = p_ref[...].astype(F32)

    def body(k, _):
        x = x_ref[:, k, :]
        twice_ref[:members] = x
        twice_ref[members:] = x
        total = jnp.zeros((members, lanes), F32)
        for d in range(1, members // 2 + 1):
            here = slope(x - twice_ref[members - d : 2 * members - d])
            total = total + here
            if 2 * d != members:
                slopes_ref[d % 2, :members] = here
                slopes_ref[d % 2, members:] = here
                total = total - slopes_ref[d % 2, d : d + members]
        sum_ref[:, k, :] = total
        return 0

    lax.fori_loop(0, deep, body, 0)
    out_ref[...] = sum_ref[...].astype(BF16)


def backward_kernel(
    channels, members, next_ref, pred_ref, obs_ref, pair_ref, hl_ref, hr_ref, wt_ref,
    up_hbm, down_hbm, head_hbm, xhat_hbm, inv_hbm, gs_hbm, ft_hbm,
    score_ref, cot_hbm, direct_hbm, out_ref,
    dpre_ref, cot_ref, direct_ref, sums_ref, x_ref,
    up_ref, down_ref, head_ref, xhat_ref, inv_ref, gs_ref, ft_ref, sems,
):
    first = start_all([(head_hbm, head_ref), (down_hbm, down_ref)], sems, 2)
    second = start_all([(gs_hbm, gs_ref)], sems, 4)
    third = start_all([(up_hbm, up_ref)], sems, 5)
    fourth = start_all([(xhat_hbm, xhat_ref), (inv_hbm, inv_ref), (ft_hbm, ft_ref)], sems, 6)
    tiles, nrows, lons, _ = xhat_ref.shape
    points = nrows * lons
    pieces, deep, _ = pred_ref.shape
    per = pieces // nrows
    for p in range(pieces):
        r, i = p // per, p % per
        rows, at = slice(i * deep, (i + 1) * deep), slice(r * lons, (r + 1) * lons)
        delta = pred_ref[p].astype(F32) - obs_ref[rows, at].astype(F32)
        score_ref[rows, at] = slope(delta) - pair_ref[p].astype(F32) * (1.0 / (members - 1))
    wait_all(first)
    mixed_cot = mm(score_ref[...].astype(BF16), head_ref[...], TN)
    rest = jnp.zeros((points, tiles * LANES - channels), F32)
    wide_cot = jnp.concatenate([mixed_cot, rest], 1).astype(BF16)
    for tile in range(tiles):
        direct_ref[tile] = wide_cot[:, cols(tile)]
    stores = start_all([(direct_ref, direct_hbm)], sems, 0)
    mixed_cot = mixed_cot.astype(BF16)
    hiddens = up_ref.shape[1]
    for start in range(0, hiddens, 256):
        stop = min(start + 256, hiddens)
        if start == 0:
            wait_all(second)
        hidden_cot = mm(mixed_cot, down_ref[:, start:stop]).astype(BF16).astype(F32)
        dpre_ref[:, start:stop] = (hidden_cot * gs_ref[:, start:stop].astype(F32)).astype(BF16)
    wait_all(third)
    normed_cot = mm(dpre_ref[...], up_ref[...], NT).astype(BF16).astype(F32)
    normed_cot = jnp.concatenate([normed_cot, rest], 1)
    wait_all(fourth)
    gains = [None] * tiles
    for r in range(nrows):
        here = slice(r * lons, (r + 1) * lons)
        first = second = None
        for tile in range(tiles):
            nc = normed_cot[here, cols(tile)]
            xhat = xhat_ref[tile, r]
            product = nc * xhat
            part = jnp.sum(product, 0, keepdims=True)
            gains[tile] = part if r == 0 else gains[tile] + part
            gain = wt_ref[tile, 49:50, :]
            scaled = nc * gain
            crossed = product * gain
            cot_ref[tile, r] = scaled
            first = scaled if first is None else first + scaled
            second = crossed if second is None else second + crossed
        first = jnp.sum(first, 1, keepdims=True) * (1.0 / channels)
        second = jnp.sum(second, 1, keepdims=True) * (1.0 / channels)
        for tile in range(tiles):
            cot_ref[tile, r] = inv_ref[r] * (cot_ref[tile, r] - first - xhat_ref[tile, r] * second)
    stores += start_all([(cot_ref, cot_hbm)], sems, 1)
    for tile in range(tiles):
        sums_ref[tile, 48:, :] = jnp.zeros((sums_ref.shape[1] - 48, LANES), F32)
        sums_ref[tile, 49:50, :] = gains[tile]


    fill_fields(x_ref, ft_ref, hl_ref, hr_ref)
    add_taps(x_ref, cot_ref, sums_ref)
    send(next_ref[0], cot_ref, sums_ref, out_ref)
    wait_all(stores)


def add_taps(x_ref, cot_ref, sums_ref):
    tiles, nrows, lons, _ = cot_ref.shape
    tall = 16

    def body(tile, _):
        for b in range(7):
            acc = [jnp.zeros((tall, LANES), F32)] * 7
            for start in range(0, lons, tall):
                at = PAD + start + b - 3
                xs = [x_ref[tile, r, at : at + tall, :] for r in range(nrows)]
                cs = [cot_ref[tile, r, start : start + tall, :] for r in range(nrows)]
                for a in range(7):
                    for r_out in range(nrows):
                        r_in = r_out + a - 3
                        if 0 <= r_in < nrows:
                            acc[a] = acc[a] + cs[r_out] * xs[r_in]
            for a in range(7):
                sums_ref[tile, a * 7 + b : a * 7 + b + 1, :] = jnp.sum(acc[a], 0, keepdims=True)
        return 0

    lax.fori_loop(0, tiles, body, 0)


def send(right, cot_ref, sums_ref, out_ref):
    tiles, nrows, _, _ = cot_ref.shape
    pieces, tall, _ = out_ref.shape
    deep = tall - 3 * nrows
    for tile in range(tiles):
        last, first = edges([cot_ref[tile, r] for r in range(nrows)])
        for p in range(pieces):
            edge = jnp.where(right == p, last, first)
            share = sums_ref[tile, p * deep : (p + 1) * deep, :]
            out_ref[p, :, cols(tile)] = jnp.concatenate([edge, share], 0).astype(BF16)


def adjoint_kernel(
    cot_hbm, hl_ref, hr_ref, wt_ref, direct_hbm, out_ref, x_ref, gather_ref, row_ref, direct_ref, sems
):
    tiles, nrows, lons, _ = cot_hbm.shape
    loads = start_all([(cot_hbm, x_ref.at[:, :, pl.ds(PAD, lons), :]), (direct_hbm, direct_ref)], sems, 0)
    channels = out_ref.shape[0]
    tall = LANES * nrows
    fill_edges(x_ref, hl_ref[...].astype(F32), hr_ref[...].astype(F32))
    target = lax.broadcasted_iota(jnp.int32, (tall, 1), 0)
    gather_ref[...] = onehot((target % nrows) * LANES + target // nrows, tall)
    wait_all(loads)

    def one(tile, count):
        for start in range(0, lons, BLOCK):
            acc = [direct_ref[tile, r * lons + start : r * lons + start + BLOCK, :].astype(F32) for r in range(nrows)]
            acc = conv_block(x_ref, wt_ref, tile, start, acc, True)
            for r in range(nrows):
                row_ref[start : start + BLOCK, cols(r)] = acc[r].astype(BF16)
        flat = mm(gather_ref[: count * nrows], row_ref[...], NT).astype(BF16)
        return flat.reshape(count, nrows, lons)

    def body(tile, _):
        out_ref[pl.ds(pl.multiple_of(tile * LANES, LANES), LANES)] = one(tile, LANES)
        return 0

    full = channels // LANES
    lax.fori_loop(0, full, body, 0)
    if full < tiles:
        got = one(full, 4 * (-(-(channels - full * LANES) // 4)))
        out_ref[full * LANES :] = got[: channels - full * LANES]


VM, HB = pltpu.VMEM, pltpu.HBM


def call(kernel, name, ins, outs, scratch=(), copies=0, flops=0, nbytes=0, mib=60):
    sems = [pltpu.SemaphoreType.DMA((copies,))] if copies else []
    return pl.pallas_call(
        kernel,
        name=name,
        out_shape=[jax.ShapeDtypeStruct(s, d) for s, d, _ in outs],
        in_specs=[pl.BlockSpec(memory_space=m) for m in ins],
        out_specs=[pl.BlockSpec(memory_space=m) for _, _, m in outs],
        scratch_shapes=[pltpu.VMEM(s, d) for s, d in scratch] + sems,
        compiler_params=params(mib),
        cost_estimate=pl.CostEstimate(flops=flops, bytes_accessed=nbytes, transcendentals=0) if nbytes else None,
    )


def pack(f):
    channels, nrows, lons = f.shape
    wide = -(-channels // LANES) * LANES
    edge = ((16, wide), BF16, VM)
    return call(
        pack_kernel, "pack", [VM], [((nrows, lons, wide), BF16, VM), edge, edge],
        [((nrows * wide, lons), F32)], mib=16,
    )(f)


def padded_shape(ft):
    nrows, lons, wide = ft.shape
    return wide // LANES, nrows, lons + 2 * PAD, LANES


def forward(members, ft, hl, hr, wt, up, down, head):
    nrows, lons, wide = ft.shape
    points = nrows * lons
    channels, hiddens = down.shape
    xhat, inv, pre = ((wide // LANES, nrows, lons, LANES), F32), ((nrows, lons, 1), F32), ((points, hiddens), F32)
    return call(
        functools.partial(forward_kernel, channels), "forward", [HB] + [VM] * 3 + [HB] * 3,
        [((members, head.shape[0] * nrows // members, lons), BF16, VM), (*xhat, HB), (*inv, HB), (*pre, HB)],
        [(padded_shape(ft), F32), ((points, wide), BF16), ((points, hiddens), BF16), xhat, inv, pre,
         (up.shape, BF16), (down.shape, BF16), (head.shape, BF16), (ft.shape, BF16)], 7,
    )(ft, hl, hr, wt, up, down, head)


def gelu_slope(pre):
    points, hiddens = pre.shape
    tall = points // 8
    return pl.pallas_call(
        slope_kernel,
        name="slope",
        grid=(8,),
        out_shape=jax.ShapeDtypeStruct(pre.shape, BF16),
        in_specs=[pl.BlockSpec((tall, hiddens), lambda i: (i, 0))],
        out_specs=pl.BlockSpec((tall, hiddens), lambda i: (i, 0)),
        compiler_params=params(),
        cost_estimate=pl.CostEstimate(flops=20 * pre.size, bytes_accessed=8 * pre.size, transcendentals=0),
    )(pre)


def backward(members, pieces, right, pred, obs, pair, hl, hr, wt, up, down, head, xhat, inv, gslope, ft):
    tiles, nrows, lons, _ = xhat.shape
    points, wide = nrows * lons, tiles * LANES
    channels, hiddens = down.shape
    sums = pieces * (4 if 4 * pieces >= 56 else 16)
    tall = 3 * nrows + sums // pieces
    direct = ((tiles, points, LANES), BF16)
    far = (up, down, head, xhat, inv, gslope, ft)
    return call(
        functools.partial(backward_kernel, channels, members), "backward", [pltpu.SMEM] + [VM] * 6 + [HB] * 7,
        [(obs.shape, F32, VM), (xhat.shape, F32, HB), (*direct, HB), ((pieces, tall, wide), BF16, VM)],
        [((points, hiddens), BF16), (xhat.shape, F32), direct, ((tiles, sums, LANES), F32), (padded_shape(ft), F32)]
        + [(v.shape, v.dtype) for v in far],
        9, 224 * xhat.size, 8 * xhat.size,
    )(right, pred, obs, pair, hl, hr, wt, *far)


def pairs(p):
    members, _, lanes = p.shape
    return call(
        pair_kernel, "pairs", [VM], [(p.shape, BF16, VM)],
        [(p.shape, F32), ((2 * members, lanes), F32), ((2, 2 * members, lanes), F32), (p.shape, F32)], mib=16,
    )(p)[0]


def adjoint(channels, cot, hl, hr, wt, direct):
    tiles, nrows, lons, _ = cot.shape
    tall = LANES * nrows
    return call(
        adjoint_kernel, "adjoint", [HB, VM, VM, VM, HB], [((channels, nrows, lons), BF16, VM)],
        [((tiles, nrows, lons + 2 * PAD, LANES), F32), ((tall, tall), BF16), ((lons, tall), BF16), (direct.shape, BF16)],
        2, 224 * cot.size, 8 * cot.size,
    )(cot, hl, hr, wt, direct)[0]


def ring(axis):
    n = lax.axis_size(axis)
    up = [(i, (i + 1) % n) for i in range(n)]
    return up, [(j, i) for i, j in up]


def swap_edges(to_right, to_left):
    up, down = ring("lon")
    return lax.ppermute(to_right, "lon", up), lax.ppermute(to_left, "lon", down)


def shards(fields, observed, conv_weight, norm_gain, up_weight, down_weight, head_weight):
    _, channels, nrows, lons = fields.shape
    nvars = observed.shape[0]
    members, pieces = lax.axis_size("ens"), lax.axis_size("lon")
    up_weight = up_weight.T
    ft, to_right, to_left = pack(fields[0])
    hl, hr = swap_edges(to_right, to_left)
    tiles = ft.shape[2] // LANES
    wt = jnp.concatenate([conv_weight.T, norm_gain[None]], 0)
    wt = jnp.pad(wt, ((0, 6), (0, tiles * LANES - channels))).reshape(56, tiles, LANES).transpose(1, 0, 2)
    pred, xhat, inv, pre = forward(members, ft, hl, hr, wt, up_weight, down_weight, head_weight)
    met = exchange(pred, "ens")
    pair = exchange(pairs(met), "ens")
    gslope = gelu_slope(pre)
    here = lax.axis_index("lon")
    before, after = (here + pieces - 1) % pieces, (here + 1) % pieces
    score, cot, direct, sent = backward(
        members, pieces, after[None], pred, observed.reshape(nvars, -1), pair, hl, hr, wt,
        up_weight, down_weight, head_weight, xhat, inv, gslope, ft,
    )
    met = exchange(sent, "lon")
    field_out, total = reduce_beside(
        jnp.sum(met[:, 3 * nrows :].astype(F32), 0).astype(BF16),
        lambda: adjoint(channels, cot, met[before], met[after], wt, direct),
    )
    return (field_out[None], score.reshape(1, nvars, nrows, lons), total[:49, :channels].T, total[49, :channels])


def exchange(x, axis):
    return lax.all_to_all(x, axis, 0, 0, tiled=True)


def reduce_beside(mine, work):
    deep, wide = mine.shape
    pieces = lax.axis_size("lon")
    parts = exchange(jnp.broadcast_to(mine, (lax.axis_size("ens"), deep, wide)), "ens")
    parts, done = lax.optimization_barrier((parts, work()))
    mine = jnp.sum(parts.astype(F32), 0).astype(BF16)
    total = exchange(jnp.broadcast_to(mine, (pieces, deep, wide)), "lon").astype(F32)
    return done, total.reshape(pieces * deep, wide)


def solution(mesh):
    in_specs = (P("ens", None, None, "lon"), P(None, None, "lon"), P(), P(), P(), P(), P())
    out_specs = (P("ens", None, None, "lon"), P("ens", None, None, "lon"), P(), P())
    return jax.shard_map(shards, mesh=mesh, in_specs=in_specs, out_specs=out_specs, check_vma=False)
```

```python
import functools
import jax
import jax.numpy as jnp
from jax import lax
from jax.experimental import pallas as pl
from jax.experimental.pallas import tpu as pltpu
from jax.sharding import PartitionSpec as P

softening = 0.0625
LANES, PAD, BLOCK = 128, 8, 32
F32, BF16 = jnp.float32, jnp.bfloat16
gelu_scale = 0.7978845608028654
gelu_cubic = 0.044715


def params(mib=60):
    return pltpu.CompilerParams(vmem_limit_bytes=mib * 1024 * 1024)


def onehot(row_target, width):
    at = lax.broadcasted_iota(jnp.int32, (row_target.shape[0], width), 1)
    return (at == row_target).astype(BF16)


NN, NT, TN = (((1,), (0,)), ((), ())), (((1,), (1,)), ((), ())), (((0,), (0,)), ((), ()))


def mm(x, y, dims=NN):
    return lax.dot_general(x, y, dims, preferred_element_type=F32)


def cols(tile):
    return slice(tile * LANES, (tile + 1) * LANES)


def edges(blocks):
    fill = [jnp.zeros((16 - 3 * len(blocks), blocks[0].shape[1]), F32)]
    last = jnp.concatenate([x[-3:] for x in blocks] + fill, 0)
    first = jnp.concatenate([x[:3] for x in blocks] + fill, 0)
    return last.astype(BF16), first.astype(BF16)


def pack_kernel(f_ref, ft_ref, right_ref, left_ref, flat_ref):
    channels, nrows, lons = f_ref.shape
    tall = LANES * nrows
    eye = onehot(lax.broadcasted_iota(jnp.int32, (lons, 1), 0), lons)
    for tile in range(ft_ref.shape[2] // LANES):
        count = min(LANES, channels - tile * LANES)
        z = f_ref[tile * LANES : tile * LANES + count].reshape(count * nrows, lons)
        if count < LANES:
            flat_ref[tile * tall :] = jnp.zeros((tall, lons), F32)
        flat_ref[tile * tall : tile * tall + count * nrows] = z.astype(F32)
        blocks = []
        for r in range(nrows):
            x = flat_ref[pl.ds(tile * tall + r, LANES, stride=nrows), :].astype(BF16)
            blocks.append(mm(eye, x, NT))
            ft_ref[r, :, cols(tile)] = blocks[r].astype(BF16)
        right_ref[:, cols(tile)], left_ref[:, cols(tile)] = edges(blocks)


def fill_edges(x_ref, left, right):
    tiles, nrows, tall, _ = x_ref.shape
    lons = tall - 2 * PAD
    for tile in range(tiles):
        for r in range(nrows):
            x_ref[tile, r, PAD - 3 : PAD, :] = left[3 * r : 3 * r + 3, cols(tile)]
            x_ref[tile, r, PAD + lons : PAD + lons + 3, :] = right[3 * r : 3 * r + 3, cols(tile)]


def fill_fields(x_ref, ft_ref, hl_ref, hr_ref):
    tiles, nrows, tall, _ = x_ref.shape
    for tile in range(tiles):
        for r in range(nrows):
            x_ref[tile, r, PAD : tall - PAD, :] = ft_ref[r, :, cols(tile)].astype(F32)
    fill_edges(x_ref, hl_ref[...].astype(F32), hr_ref[...].astype(F32))


def start_all(pairs_of_refs, sems, first):
    copies = [pltpu.make_async_copy(a, b, sems.at[first + i]) for i, (a, b) in enumerate(pairs_of_refs)]
    for copy in copies:
        copy.start()
    return copies


def wait_all(copies):
    for copy in copies:
        copy.wait()


def conv_block(x_ref, wt_ref, tile, start, acc, flip):
    nrows = len(acc)
    tall = acc[0].shape[0]
    acc = [v.reshape(tall // 8, 8, LANES) for v in acc]
    for b in range(7):
        at = PAD + start + (3 - b if flip else b - 3)
        xs = [x_ref[tile, r, at : at + tall, :].reshape(tall // 8, 8, LANES) for r in range(nrows)]
        for a in range(7):
            w = wt_ref[tile, pl.ds(a * 7 + b, 8, stride=0), :][None]
            for r_out in range(nrows):
                r_in = r_out + a - 3
                if 0 <= r_in < nrows:
                    to, of = (r_in, r_out) if flip else (r_out, r_in)
                    acc[to] = acc[to] + w * xs[of]
    return [v.reshape(tall, LANES) for v in acc]


def forward_kernel(
    channels, ft_hbm, hl_ref, hr_ref, wt_ref, up_hbm, down_hbm, head_hbm,
    pred_ref, xhat_hbm, inv_hbm, pre_hbm,
    x_ref, normed_ref, hidden_ref, xhat_ref, inv_ref, pre_ref, up_ref, down_ref, head_ref, ft_ref, sems,
):
    fields = start_all([(ft_hbm, ft_ref)], sems, 6)
    loads = start_all([(up_hbm, up_ref), (down_hbm, down_ref), (head_hbm, head_ref)], sems, 0)
    nrows, lons, wide = ft_ref.shape
    tiles = wide // LANES
    wait_all(fields)
    fill_fields(x_ref, ft_ref, hl_ref, hr_ref)

    def conv(tile, _):
        for start in range(0, lons, BLOCK):
            acc = conv_block(x_ref, wt_ref, tile, start, [jnp.zeros((BLOCK, LANES), F32)] * nrows, False)
            for r in range(nrows):
                xhat_ref[tile, r, start : start + BLOCK, :] = acc[r]
        return 0

    lax.fori_loop(0, tiles, conv, 0)
    for r in range(nrows):
        total = xhat_ref[0, r]
        for tile in range(1, tiles):
            total = total + xhat_ref[tile, r]
        mean = jnp.sum(total, 1, keepdims=True) * (1.0 / channels)
        total = None
        for tile in range(tiles):
            offset = xhat_ref[tile, r] - mean
            xhat_ref[tile, r] = offset
            square = offset * offset
            live = channels - tile * LANES
            if live < LANES:
                square = jnp.where(lax.broadcasted_iota(jnp.int32, square.shape, 1) < live, square, 0.0)
            total = square if total is None else total + square
        inv = lax.rsqrt(jnp.sum(total, 1, keepdims=True) * (1.0 / channels) + 1e-05)
        inv_ref[r] = inv
        for tile in range(tiles):
            xhat = xhat_ref[tile, r] * inv
            xhat_ref[tile, r] = xhat
            gain = wt_ref[tile, 49:50, :]
            normed_ref[r * lons : (r + 1) * lons, cols(tile)] = (xhat * gain).astype(BF16)
    stores = start_all([(xhat_ref, xhat_hbm), (inv_ref, inv_hbm)], sems, 3)
    wait_all(loads)
    hiddens = up_ref.shape[1]
    normed = normed_ref[:, :channels]
    for start in range(0, hiddens, 256):
        stop = min(start + 256, hiddens)
        pre = mm(normed, up_ref[:, start:stop])
        pre_ref[:, start:stop] = pre
        t = jnp.tanh(pre * (gelu_scale + (gelu_scale * gelu_cubic) * (pre * pre)))
        hidden_ref[:, start:stop] = (pre * (0.5 + 0.5 * t)).astype(BF16)
    stores += start_all([(pre_ref, pre_hbm)], sems, 5)
    lift = mm(hidden_ref[...], down_ref[...], NT)
    own = jnp.concatenate([ft_ref[r, :, :channels] for r in range(nrows)], axis=0)
    mixed = (own.astype(F32) + lift).astype(BF16)
    pred = mm(head_ref[...], mixed, NT).astype(BF16)
    pieces, deep, _ = pred_ref.shape
    per = pieces // nrows
    for p in range(pieces):
        r, i = p // per, p % per
        pred_ref[p] = pred[i * deep : (i + 1) * deep, r * lons : (r + 1) * lons]
    wait_all(stores)


def slope_kernel(pre_ref, out_ref):
    def body(i, _):
        at = pl.ds(pl.multiple_of(i * 16, 16), 16)
        pre = pre_ref[at, :]
        square = pre * pre
        t = jnp.tanh(pre * (gelu_scale + (gelu_scale * gelu_cubic) * square))
        half = 0.5 + 0.5 * t
        bend = 0.5 * gelu_scale + (1.5 * gelu_scale * gelu_cubic) * square
        out_ref[at, :] = (half + pre * (1.0 - t * t) * bend).astype(BF16)
        return 0

    lax.fori_loop(0, pre_ref.shape[0] // 16, body, 0)


def slope(delta):
    return delta * lax.rsqrt(delta * delta + softening)


def pair_kernel(p_ref, out_ref, x_ref, twice_ref, slopes_ref, sum_ref):
    members, deep, lanes = p_ref.shape
    x_ref[...] = p_ref[...].astype(F32)

    def body(k, _):
        x = x_ref[:, k, :]
        twice_ref[:members] = x
        twice_ref[members:] = x
        total = jnp.zeros((members, lanes), F32)
        for d in range(1, members // 2 + 1):
            here = slope(x - twice_ref[members - d : 2 * members - d])
            total = total + here
            if 2 * d != members:
                slopes_ref[d % 2, :members] = here
                slopes_ref[d % 2, members:] = here
                total = total - slopes_ref[d % 2, d : d + members]
        sum_ref[:, k, :] = total
        return 0

    lax.fori_loop(0, deep, body, 0)
    out_ref[...] = sum_ref[...].astype(BF16)


def backward_kernel(
    channels, members, pred_ref, obs_ref, pair_ref, hl_ref, hr_ref, wt_ref,
    up_hbm, down_hbm, head_hbm, xhat_hbm, inv_hbm, gs_hbm, ft_hbm,
    score_ref, cot_hbm, direct_hbm, right_ref, left_ref, out_ref,
    dpre_ref, cot_ref, direct_ref, sums_ref, x_ref,
    up_ref, down_ref, head_ref, xhat_ref, inv_ref, gs_ref, ft_ref, sems,
):
    first = start_all([(head_hbm, head_ref), (down_hbm, down_ref)], sems, 2)
    second = start_all([(gs_hbm, gs_ref)], sems, 4)
    third = start_all([(up_hbm, up_ref)], sems, 5)
    fourth = start_all([(xhat_hbm, xhat_ref), (inv_hbm, inv_ref), (ft_hbm, ft_ref)], sems, 6)
    tiles, nrows, lons, _ = xhat_ref.shape
    points = nrows * lons
    pieces, deep, _ = pred_ref.shape
    per = pieces // nrows
    for p in range(pieces):
        r, i = p // per, p % per
        rows, at = slice(i * deep, (i + 1) * deep), slice(r * lons, (r + 1) * lons)
        delta = pred_ref[p].astype(F32) - obs_ref[rows, at].astype(F32)
        score_ref[rows, at] = slope(delta) - pair_ref[p].astype(F32) * (1.0 / (members - 1))
    wait_all(first)
    mixed_cot = mm(score_ref[...].astype(BF16), head_ref[...], TN)
    rest = jnp.zeros((points, tiles * LANES - channels), F32)
    wide_cot = jnp.concatenate([mixed_cot, rest], 1).astype(BF16)
    for tile in range(tiles):
        direct_ref[tile] = wide_cot[:, cols(tile)]
    stores = start_all([(direct_ref, direct_hbm)], sems, 0)
    mixed_cot = mixed_cot.astype(BF16)
    hiddens = up_ref.shape[1]
    for start in range(0, hiddens, 256):
        stop = min(start + 256, hiddens)
        if start == 0:
            wait_all(second)
        hidden_cot = mm(mixed_cot, down_ref[:, start:stop]).astype(BF16).astype(F32)
        dpre_ref[:, start:stop] = (hidden_cot * gs_ref[:, start:stop].astype(F32)).astype(BF16)
    wait_all(third)
    normed_cot = mm(dpre_ref[...], up_ref[...], NT).astype(BF16).astype(F32)
    normed_cot = jnp.concatenate([normed_cot, rest], 1)
    wait_all(fourth)
    gains = [None] * tiles
    for r in range(nrows):
        here = slice(r * lons, (r + 1) * lons)
        first = second = None
        for tile in range(tiles):
            nc = normed_cot[here, cols(tile)]
            xhat = xhat_ref[tile, r]
            product = nc * xhat
            part = jnp.sum(product, 0, keepdims=True)
            gains[tile] = part if r == 0 else gains[tile] + part
            gain = wt_ref[tile, 49:50, :]
            scaled = nc * gain
            crossed = product * gain
            cot_ref[tile, r] = scaled
            first = scaled if first is None else first + scaled
            second = crossed if second is None else second + crossed
        first = jnp.sum(first, 1, keepdims=True) * (1.0 / channels)
        second = jnp.sum(second, 1, keepdims=True) * (1.0 / channels)
        for tile in range(tiles):
            cot_ref[tile, r] = inv_ref[r] * (cot_ref[tile, r] - first - xhat_ref[tile, r] * second)
    stores += start_all([(cot_ref, cot_hbm)], sems, 1)
    for tile in range(tiles):
        sums_ref[tile, 48:, :] = jnp.zeros((sums_ref.shape[1] - 48, LANES), F32)
        sums_ref[tile, 49:50, :] = gains[tile]
        right_ref[:, cols(tile)], left_ref[:, cols(tile)] = edges([cot_ref[tile, r] for r in range(nrows)])


    fill_fields(x_ref, ft_ref, hl_ref, hr_ref)
    add_taps(x_ref, cot_ref, sums_ref)
    pieces, deep, _ = out_ref.shape
    for tile in range(tiles):
        for p in range(pieces):
            out_ref[p, :, cols(tile)] = sums_ref[tile, p * deep : (p + 1) * deep, :].astype(BF16)
    wait_all(stores)


def add_taps(x_ref, cot_ref, sums_ref):
    tiles, nrows, lons, _ = cot_ref.shape
    tall = 16

    def body(tile, _):
        for b in range(7):
            acc = [jnp.zeros((tall, LANES), F32)] * 7
            for start in range(0, lons, tall):
                at = PAD + start + b - 3
                xs = [x_ref[tile, r, at : at + tall, :] for r in range(nrows)]
                cs = [cot_ref[tile, r, start : start + tall, :] for r in range(nrows)]
                for a in range(7):
                    for r_out in range(nrows):
                        r_in = r_out + a - 3
                        if 0 <= r_in < nrows:
                            acc[a] = acc[a] + cs[r_out] * xs[r_in]
            for a in range(7):
                sums_ref[tile, a * 7 + b : a * 7 + b + 1, :] = jnp.sum(acc[a], 0, keepdims=True)
        return 0

    lax.fori_loop(0, tiles, body, 0)


def adjoint_kernel(
    cot_hbm, hl_ref, hr_ref, wt_ref, direct_hbm, out_ref, x_ref, gather_ref, row_ref, direct_ref, sems
):
    tiles, nrows, lons, _ = cot_hbm.shape
    loads = start_all([(cot_hbm, x_ref.at[:, :, pl.ds(PAD, lons), :]), (direct_hbm, direct_ref)], sems, 0)
    channels = out_ref.shape[0]
    tall = LANES * nrows
    fill_edges(x_ref, hl_ref[...].astype(F32), hr_ref[...].astype(F32))
    target = lax.broadcasted_iota(jnp.int32, (tall, 1), 0)
    gather_ref[...] = onehot((target % nrows) * LANES + target // nrows, tall)
    wait_all(loads)

    def one(tile, count):
        for start in range(0, lons, BLOCK):
            acc = [direct_ref[tile, r * lons + start : r * lons + start + BLOCK, :].astype(F32) for r in range(nrows)]
            acc = conv_block(x_ref, wt_ref, tile, start, acc, True)
            for r in range(nrows):
                row_ref[start : start + BLOCK, cols(r)] = acc[r].astype(BF16)
        flat = mm(gather_ref[: count * nrows], row_ref[...], NT).astype(BF16)
        return flat.reshape(count, nrows, lons)

    def body(tile, _):
        out_ref[pl.ds(pl.multiple_of(tile * LANES, LANES), LANES)] = one(tile, LANES)
        return 0

    full = channels // LANES
    lax.fori_loop(0, full, body, 0)
    if full < tiles:
        got = one(full, 4 * (-(-(channels - full * LANES) // 4)))
        out_ref[full * LANES :] = got[: channels - full * LANES]


VM, HB = pltpu.VMEM, pltpu.HBM


def call(kernel, name, ins, outs, scratch=(), copies=0, flops=0, nbytes=0, mib=60):
    sems = [pltpu.SemaphoreType.DMA((copies,))] if copies else []
    return pl.pallas_call(
        kernel,
        name=name,
        out_shape=[jax.ShapeDtypeStruct(s, d) for s, d, _ in outs],
        in_specs=[pl.BlockSpec(memory_space=m) for m in ins],
        out_specs=[pl.BlockSpec(memory_space=m) for _, _, m in outs],
        scratch_shapes=[pltpu.VMEM(s, d) for s, d in scratch] + sems,
        compiler_params=params(mib),
        cost_estimate=pl.CostEstimate(flops=flops, bytes_accessed=nbytes, transcendentals=0) if nbytes else None,
    )


def pack(f):
    channels, nrows, lons = f.shape
    wide = -(-channels // LANES) * LANES
    edge = ((16, wide), BF16, VM)
    return call(
        pack_kernel, "pack", [VM], [((nrows, lons, wide), BF16, VM), edge, edge],
        [((nrows * wide, lons), F32)], mib=16,
    )(f)


def padded_shape(ft):
    nrows, lons, wide = ft.shape
    return wide // LANES, nrows, lons + 2 * PAD, LANES


def forward(members, ft, hl, hr, wt, up, down, head):
    nrows, lons, wide = ft.shape
    points = nrows * lons
    channels, hiddens = down.shape
    xhat, inv, pre = ((wide // LANES, nrows, lons, LANES), F32), ((nrows, lons, 1), F32), ((points, hiddens), F32)
    return call(
        functools.partial(forward_kernel, channels), "forward", [HB] + [VM] * 3 + [HB] * 3,
        [((members, head.shape[0] * nrows // members, lons), BF16, VM), (*xhat, HB), (*inv, HB), (*pre, HB)],
        [(padded_shape(ft), F32), ((points, wide), BF16), ((points, hiddens), BF16), xhat, inv, pre,
         (up.shape, BF16), (down.shape, BF16), (head.shape, BF16), (ft.shape, BF16)], 7,
    )(ft, hl, hr, wt, up, down, head)


def gelu_slope(pre):
    points, hiddens = pre.shape
    tall = points // 8
    return pl.pallas_call(
        slope_kernel,
        name="slope",
        grid=(8,),
        out_shape=jax.ShapeDtypeStruct(pre.shape, BF16),
        in_specs=[pl.BlockSpec((tall, hiddens), lambda i: (i, 0))],
        out_specs=pl.BlockSpec((tall, hiddens), lambda i: (i, 0)),
        compiler_params=params(),
        cost_estimate=pl.CostEstimate(flops=20 * pre.size, bytes_accessed=8 * pre.size, transcendentals=0),
    )(pre)


def backward(members, pieces, pred, obs, pair, hl, hr, wt, up, down, head, xhat, inv, gslope, ft):
    tiles, nrows, lons, _ = xhat.shape
    points, wide = nrows * lons, tiles * LANES
    channels, hiddens = down.shape
    sums = pieces * (4 if 4 * pieces >= 56 else 16)
    edge = ((16, wide), BF16, VM)
    direct = ((tiles, points, LANES), BF16)
    far = (up, down, head, xhat, inv, gslope, ft)
    return call(
        functools.partial(backward_kernel, channels, members), "backward", [VM] * 6 + [HB] * 7,
        [(obs.shape, F32, VM), (xhat.shape, F32, HB), (*direct, HB), edge, edge, ((pieces, sums // pieces, wide), BF16, VM)],
        [((points, hiddens), BF16), (xhat.shape, F32), direct, ((tiles, sums, LANES), F32), (padded_shape(ft), F32)]
        + [(v.shape, v.dtype) for v in far],
        9, 224 * xhat.size, 8 * xhat.size,
    )(pred, obs, pair, hl, hr, wt, *far)


def pairs(p):
    members, _, lanes = p.shape
    return call(
        pair_kernel, "pairs", [VM], [(p.shape, BF16, VM)],
        [(p.shape, F32), ((2 * members, lanes), F32), ((2, 2 * members, lanes), F32), (p.shape, F32)], mib=16,
    )(p)[0]


def adjoint(channels, cot, hl, hr, wt, direct):
    tiles, nrows, lons, _ = cot.shape
    tall = LANES * nrows
    return call(
        adjoint_kernel, "adjoint", [HB, VM, VM, VM, HB], [((channels, nrows, lons), BF16, VM)],
        [((tiles, nrows, lons + 2 * PAD, LANES), F32), ((tall, tall), BF16), ((lons, tall), BF16), (direct.shape, BF16)],
        2, 224 * cot.size, 8 * cot.size,
    )(cot, hl, hr, wt, direct)[0]


def ring(axis):
    n = lax.axis_size(axis)
    up = [(i, (i + 1) % n) for i in range(n)]
    return up, [(j, i) for i, j in up]


def swap_edges(to_right, to_left):
    up, down = ring("lon")
    return lax.ppermute(to_right, "lon", up), lax.ppermute(to_left, "lon", down)


def shards(fields, observed, conv_weight, norm_gain, up_weight, down_weight, head_weight):
    _, channels, nrows, lons = fields.shape
    nvars = observed.shape[0]
    members, pieces = lax.axis_size("ens"), lax.axis_size("lon")
    up_weight = up_weight.T
    ft, to_right, to_left = pack(fields[0])
    hl, hr = swap_edges(to_right, to_left)
    tiles = ft.shape[2] // LANES
    wt = jnp.concatenate([conv_weight.T, norm_gain[None]], 0)
    wt = jnp.pad(wt, ((0, 6), (0, tiles * LANES - channels))).reshape(56, tiles, LANES).transpose(1, 0, 2)
    pred, xhat, inv, pre = forward(members, ft, hl, hr, wt, up_weight, down_weight, head_weight)
    met = exchange(pred, "ens")
    pair = exchange(pairs(met), "ens")
    gslope = gelu_slope(pre)
    score, cot, direct, to_right, to_left, shares = backward(
        members, pieces, pred, observed.reshape(nvars, -1), pair, hl, hr, wt,
        up_weight, down_weight, head_weight, xhat, inv, gslope, ft,
    )
    field_out, total = reduce_beside(
        shares, swap_edges(to_right, to_left), lambda cl, cr: adjoint(channels, cot, cl, cr, wt, direct)
    )
    return (field_out[None], score.reshape(1, nvars, nrows, lons), total[:49, :channels].T, total[49, :channels])


def exchange(x, axis):
    return lax.all_to_all(x, axis, 0, 0, tiled=True)


def reduce_beside(shares, edges_in, work):
    pieces, deep, wide = shares.shape
    parts, edges_in = lax.optimization_barrier((exchange(shares, "lon"), edges_in))
    mine = jnp.sum(parts.astype(F32), 0).astype(BF16)
    parts = exchange(jnp.broadcast_to(mine, (lax.axis_size("ens"), deep, wide)), "ens")
    parts, done = lax.optimization_barrier((parts, work(*edges_in)))
    mine = jnp.sum(parts.astype(F32), 0).astype(BF16)
    total = exchange(jnp.broadcast_to(mine, (pieces, deep, wide)), "lon").astype(F32)
    return done, total.reshape(pieces * deep, wide)


def solution(mesh):
    in_specs = (P("ens", None, None, "lon"), P(None, None, "lon"), P(), P(), P(), P(), P())
    out_specs = (P("ens", None, None, "lon"), P("ens", None, None, "lon"), P(), P())
    return jax.shard_map(shards, mesh=mesh, in_specs=in_specs, out_specs=out_specs, check_vma=False)
```

```python
import functools
import jax
import jax.numpy as jnp
from jax import lax
from jax.experimental import pallas as pl
from jax.experimental.pallas import tpu as pltpu
from jax.sharding import PartitionSpec as P

softening = 0.0625
LANES, PAD, BLOCK = 128, 8, 32
F32, BF16 = jnp.float32, jnp.bfloat16
gelu_scale = 0.7978845608028654
gelu_cubic = 0.044715


def params(mib=60):
    return pltpu.CompilerParams(vmem_limit_bytes=mib * 1024 * 1024)


def onehot(row_target, width):
    at = lax.broadcasted_iota(jnp.int32, (row_target.shape[0], width), 1)
    return (at == row_target).astype(BF16)


NN, NT, TN = (((1,), (0,)), ((), ())), (((1,), (1,)), ((), ())), (((0,), (0,)), ((), ()))


def mm(x, y, dims=NN):
    return lax.dot_general(x, y, dims, preferred_element_type=F32)


def cols(tile):
    return slice(tile * LANES, (tile + 1) * LANES)


def edges(blocks):
    return jnp.concatenate([x[-3:] for x in blocks], 0), jnp.concatenate([x[:3] for x in blocks], 0)


def pack_kernel(f_ref, ft_ref, right_ref, left_ref, flat_ref):
    channels, nrows, lons = f_ref.shape
    tall = LANES * nrows
    eye = onehot(lax.broadcasted_iota(jnp.int32, (lons, 1), 0), lons)
    for tile in range(ft_ref.shape[2] // LANES):
        count = min(LANES, channels - tile * LANES)
        z = f_ref[tile * LANES : tile * LANES + count].reshape(count * nrows, lons)
        if count < LANES:
            flat_ref[tile * tall :] = jnp.zeros((tall, lons), F32)
        flat_ref[tile * tall : tile * tall + count * nrows] = z.astype(F32)
        blocks = []
        for r in range(nrows):
            x = flat_ref[pl.ds(tile * tall + r, LANES, stride=nrows), :].astype(BF16)
            blocks.append(mm(eye, x, NT))
            ft_ref[r, :, cols(tile)] = blocks[r].astype(BF16)
        fill = jnp.zeros((16 - 3 * nrows, LANES), F32)
        last, first = edges(blocks)
        right_ref[:, cols(tile)] = jnp.concatenate([last, fill], 0).astype(BF16)
        left_ref[:, cols(tile)] = jnp.concatenate([first, fill], 0).astype(BF16)


def fill_edges(x_ref, left, right):
    tiles, nrows, tall, _ = x_ref.shape
    lons = tall - 2 * PAD
    for tile in range(tiles):
        for r in range(nrows):
            x_ref[tile, r, PAD - 3 : PAD, :] = left[3 * r : 3 * r + 3, cols(tile)]
            x_ref[tile, r, PAD + lons : PAD + lons + 3, :] = right[3 * r : 3 * r + 3, cols(tile)]


def fill_fields(x_ref, ft_ref, hl_ref, hr_ref):
    tiles, nrows, tall, _ = x_ref.shape
    for tile in range(tiles):
        for r in range(nrows):
            x_ref[tile, r, PAD : tall - PAD, :] = ft_ref[r, :, cols(tile)].astype(F32)
    fill_edges(x_ref, hl_ref[...].astype(F32), hr_ref[...].astype(F32))


def start_all(pairs_of_refs, sems, first):
    copies = [pltpu.make_async_copy(a, b, sems.at[first + i]) for i, (a, b) in enumerate(pairs_of_refs)]
    for copy in copies:
        copy.start()
    return copies


def wait_all(copies):
    for copy in copies:
        copy.wait()


def conv_block(x_ref, wt_ref, tile, start, acc, flip):
    nrows = len(acc)
    tall = acc[0].shape[0]
    acc = [v.reshape(tall // 8, 8, LANES) for v in acc]
    for b in range(7):
        at = PAD + start + (3 - b if flip else b - 3)
        xs = [x_ref[tile, r, at : at + tall, :].reshape(tall // 8, 8, LANES) for r in range(nrows)]
        for a in range(7):
            w = wt_ref[tile, pl.ds(a * 7 + b, 8, stride=0), :][None]
            for r_out in range(nrows):
                r_in = r_out + a - 3
                if 0 <= r_in < nrows:
                    to, of = (r_in, r_out) if flip else (r_out, r_in)
                    acc[to] = acc[to] + w * xs[of]
    return [v.reshape(tall, LANES) for v in acc]


def forward_kernel(
    channels, ft_hbm, hl_hbm, hr_hbm, wt_hbm, up_hbm, down_hbm, head_hbm,
    pred_ref, xhat_hbm, inv_hbm, pre_hbm,
    x_ref, normed_ref, hidden_ref, xhat_ref, inv_ref, pre_ref, up_ref, down_ref, head_ref, ft_ref, hl_ref, hr_ref, wt_ref, sems,
):
    fields = start_all([(hl_hbm, hl_ref), (hr_hbm, hr_ref), (ft_hbm, ft_ref), (wt_hbm, wt_ref)], sems, 6)
    loads = start_all([(up_hbm, up_ref), (down_hbm, down_ref), (head_hbm, head_ref)], sems, 0)
    nrows, lons, wide = ft_ref.shape
    tiles = wide // LANES
    wait_all(fields)
    fill_fields(x_ref, ft_ref, hl_ref, hr_ref)

    def conv(tile, _):
        for start in range(0, lons, BLOCK):
            acc = conv_block(x_ref, wt_ref, tile, start, [jnp.zeros((BLOCK, LANES), F32)] * nrows, False)
            for r in range(nrows):
                xhat_ref[tile, r, start : start + BLOCK, :] = acc[r]
        return 0

    lax.fori_loop(0, tiles, conv, 0)
    for r in range(nrows):
        total = xhat_ref[0, r]
        for tile in range(1, tiles):
            total = total + xhat_ref[tile, r]
        mean = jnp.sum(total, 1, keepdims=True) * (1.0 / channels)
        total = None
        for tile in range(tiles):
            offset = xhat_ref[tile, r] - mean
            xhat_ref[tile, r] = offset
            square = offset * offset
            live = channels - tile * LANES
            if live < LANES:
                square = jnp.where(lax.broadcasted_iota(jnp.int32, square.shape, 1) < live, square, 0.0)
            total = square if total is None else total + square
        inv = lax.rsqrt(jnp.sum(total, 1, keepdims=True) * (1.0 / channels) + 1e-05)
        inv_ref[r] = inv
        for tile in range(tiles):
            xhat = xhat_ref[tile, r] * inv
            xhat_ref[tile, r] = xhat
            gain = wt_ref[tile, 49:50, :]
            normed_ref[r * lons : (r + 1) * lons, cols(tile)] = (xhat * gain).astype(BF16)
    stores = start_all([(xhat_ref, xhat_hbm), (inv_ref, inv_hbm)], sems, 3)
    wait_all(loads)
    hiddens = up_ref.shape[1]
    normed = normed_ref[:, :channels]
    for start in range(0, hiddens, 256):
        stop = min(start + 256, hiddens)
        pre = mm(normed, up_ref[:, start:stop])
        pre_ref[:, start:stop] = pre
        t = jnp.tanh(pre * (gelu_scale + (gelu_scale * gelu_cubic) * (pre * pre)))
        hidden_ref[:, start:stop] = (pre * (0.5 + 0.5 * t)).astype(BF16)
    stores += start_all([(pre_ref, pre_hbm)], sems, 5)
    lift = mm(hidden_ref[...], down_ref[...], NT)
    own = jnp.concatenate([ft_ref[r, :, :channels] for r in range(nrows)], axis=0)
    mixed = (own.astype(F32) + lift).astype(BF16)
    pred = mm(head_ref[...], mixed, NT).astype(BF16)
    pieces, deep, _ = pred_ref.shape
    per = pieces // nrows
    for p in range(pieces):
        r, i = p // per, p % per
        pred_ref[p] = pred[i * deep : (i + 1) * deep, r * lons : (r + 1) * lons]
    wait_all(stores)


def slope_kernel(pre_ref, out_ref):
    def body(i, _):
        at = pl.ds(pl.multiple_of(i * 16, 16), 16)
        pre = pre_ref[at, :]
        square = pre * pre
        t = jnp.tanh(pre * (gelu_scale + (gelu_scale * gelu_cubic) * square))
        half = 0.5 + 0.5 * t
        bend = 0.5 * gelu_scale + (1.5 * gelu_scale * gelu_cubic) * square
        out_ref[at, :] = (half + pre * (1.0 - t * t) * bend).astype(BF16)
        return 0

    lax.fori_loop(0, pre_ref.shape[0] // 16, body, 0)


def slope(delta):
    return delta * lax.rsqrt(delta * delta + softening)


def pair_kernel(p_ref, out_ref, x_ref, twice_ref, slopes_ref, sum_ref):
    members, deep, lanes = p_ref.shape
    x_ref[...] = p_ref[...].astype(F32)

    def body(k, _):
        x = x_ref[:, k, :]
        twice_ref[:members] = x
        twice_ref[members:] = x
        total = jnp.zeros((members, lanes), F32)
        for d in range(1, members // 2 + 1):
            here = slope(x - twice_ref[members - d : 2 * members - d])
            total = total + here
            if 2 * d != members:
                slopes_ref[d % 2, :members] = here
                slopes_ref[d % 2, members:] = here
                total = total - slopes_ref[d % 2, d : d + members]
        sum_ref[:, k, :] = total
        return 0

    lax.fori_loop(0, deep, body, 0)
    out_ref[...] = sum_ref[...].astype(BF16)


def backward_kernel(
    channels, members, next_ref, pred_hbm, obs_hbm, pair_hbm, hl_hbm, hr_hbm, wt_hbm,
    up_hbm, down_hbm, head_hbm, xhat_hbm, inv_hbm, gs_hbm, ft_hbm,
    score_ref, cot_hbm, direct_hbm, out_ref,
    dpre_ref, cot_ref, direct_ref, sums_ref, x_ref,
    pred_ref, obs_ref, pair_ref, hl_ref, hr_ref, wt_ref,
    up_ref, down_ref, head_ref, xhat_ref, inv_ref, gs_ref, ft_ref, sems,
):
    small = start_all([(pred_hbm, pred_ref), (obs_hbm, obs_ref), (pair_hbm, pair_ref)], sems, 9)
    first = start_all([(head_hbm, head_ref), (down_hbm, down_ref)], sems, 2)
    second = start_all([(gs_hbm, gs_ref)], sems, 4)
    third = start_all([(up_hbm, up_ref)], sems, 5)
    fourth = start_all([(xhat_hbm, xhat_ref), (inv_hbm, inv_ref), (ft_hbm, ft_ref)], sems, 6)
    fourth += start_all([(hl_hbm, hl_ref), (hr_hbm, hr_ref), (wt_hbm, wt_ref)], sems, 12)
    wait_all(small)
    tiles, nrows, lons, _ = xhat_ref.shape
    points = nrows * lons
    pieces, deep, _ = pred_ref.shape
    per = pieces // nrows
    for p in range(pieces):
        r, i = p // per, p % per
        rows, at = slice(i * deep, (i + 1) * deep), slice(r * lons, (r + 1) * lons)
        delta = pred_ref[p].astype(F32) - obs_ref[rows, at].astype(F32)
        score_ref[rows, at] = slope(delta) - pair_ref[p].astype(F32) * (1.0 / (members - 1))
    wait_all(first)
    mixed_cot = mm(score_ref[...].astype(BF16), head_ref[...], TN)
    rest = jnp.zeros((points, tiles * LANES - channels), F32)
    wide_cot = jnp.concatenate([mixed_cot, rest], 1).astype(BF16)
    for tile in range(tiles):
        direct_ref[tile] = wide_cot[:, cols(tile)]
    stores = start_all([(direct_ref, direct_hbm)], sems, 0)
    mixed_cot = mixed_cot.astype(BF16)
    hiddens = up_ref.shape[1]
    for start in range(0, hiddens, 256):
        stop = min(start + 256, hiddens)
        if start == 0:
            wait_all(second)
        hidden_cot = mm(mixed_cot, down_ref[:, start:stop]).astype(BF16).astype(F32)
        dpre_ref[:, start:stop] = (hidden_cot * gs_ref[:, start:stop].astype(F32)).astype(BF16)
    wait_all(third)
    normed_cot = mm(dpre_ref[...], up_ref[...], NT).astype(BF16).astype(F32)
    normed_cot = jnp.concatenate([normed_cot, rest], 1)
    wait_all(fourth)
    gains = [None] * tiles
    for r in range(nrows):
        here = slice(r * lons, (r + 1) * lons)
        first = second = None
        for tile in range(tiles):
            nc = normed_cot[here, cols(tile)]
            xhat = xhat_ref[tile, r]
            product = nc * xhat
            part = jnp.sum(product, 0, keepdims=True)
            gains[tile] = part if r == 0 else gains[tile] + part
            gain = wt_ref[tile, 49:50, :]
            scaled = nc * gain
            crossed = product * gain
            cot_ref[tile, r] = scaled
            first = scaled if first is None else first + scaled
            second = crossed if second is None else second + crossed
        first = jnp.sum(first, 1, keepdims=True) * (1.0 / channels)
        second = jnp.sum(second, 1, keepdims=True) * (1.0 / channels)
        for tile in range(tiles):
            cot_ref[tile, r] = inv_ref[r] * (cot_ref[tile, r] - first - xhat_ref[tile, r] * second)
    stores += start_all([(cot_ref, cot_hbm)], sems, 1)
    for tile in range(tiles):
        sums_ref[tile, 48:, :] = jnp.zeros((sums_ref.shape[1] - 48, LANES), F32)
        sums_ref[tile, 49:50, :] = gains[tile]


    fill_fields(x_ref, ft_ref, hl_ref, hr_ref)
    add_taps(x_ref, cot_ref, sums_ref)
    send(next_ref[0], cot_ref, sums_ref, out_ref)
    wait_all(stores)


def add_taps(x_ref, cot_ref, sums_ref):
    tiles, nrows, lons, _ = cot_ref.shape
    tall = 16

    def body(tile, _):
        for b in range(7):
            acc = [jnp.zeros((tall, LANES), F32)] * 7
            for start in range(0, lons, tall):
                at = PAD + start + b - 3
                xs = [x_ref[tile, r, at : at + tall, :] for r in range(nrows)]
                cs = [cot_ref[tile, r, start : start + tall, :] for r in range(nrows)]
                for a in range(7):
                    for r_out in range(nrows):
                        r_in = r_out + a - 3
                        if 0 <= r_in < nrows:
                            acc[a] = acc[a] + cs[r_out] * xs[r_in]
            for a in range(7):
                sums_ref[tile, a * 7 + b : a * 7 + b + 1, :] = jnp.sum(acc[a], 0, keepdims=True)
        return 0

    lax.fori_loop(0, tiles, body, 0)


def send(right, cot_ref, sums_ref, out_ref):
    tiles, nrows, _, _ = cot_ref.shape
    pieces, tall, _ = out_ref.shape
    deep = tall - 3 * nrows
    for tile in range(tiles):
        last, first = edges([cot_ref[tile, r] for r in range(nrows)])
        for p in range(pieces):
            edge = jnp.where(right == p, last, first)
            share = sums_ref[tile, p * deep : (p + 1) * deep, :]
            out_ref[p, :, cols(tile)] = jnp.concatenate([edge, share], 0).astype(BF16)


def adjoint_kernel(
    cot_hbm, hl_ref, hr_ref, wt_ref, direct_hbm, out_ref, x_ref, gather_ref, row_ref, direct_ref, sems
):
    tiles, nrows, lons, _ = cot_hbm.shape
    loads = start_all([(cot_hbm, x_ref.at[:, :, pl.ds(PAD, lons), :]), (direct_hbm, direct_ref)], sems, 0)
    channels = out_ref.shape[0]
    tall = LANES * nrows
    fill_edges(x_ref, hl_ref[...].astype(F32), hr_ref[...].astype(F32))
    target = lax.broadcasted_iota(jnp.int32, (tall, 1), 0)
    gather_ref[...] = onehot((target % nrows) * LANES + target // nrows, tall)
    wait_all(loads)

    def one(tile, count):
        for start in range(0, lons, BLOCK):
            acc = [direct_ref[tile, r * lons + start : r * lons + start + BLOCK, :].astype(F32) for r in range(nrows)]
            acc = conv_block(x_ref, wt_ref, tile, start, acc, True)
            for r in range(nrows):
                row_ref[start : start + BLOCK, cols(r)] = acc[r].astype(BF16)
        flat = mm(gather_ref[: count * nrows], row_ref[...], NT).astype(BF16)
        return flat.reshape(count, nrows, lons)

    def body(tile, _):
        out_ref[pl.ds(pl.multiple_of(tile * LANES, LANES), LANES)] = one(tile, LANES)
        return 0

    full = channels // LANES
    lax.fori_loop(0, full, body, 0)
    if full < tiles:
        got = one(full, 4 * (-(-(channels - full * LANES) // 4)))
        out_ref[full * LANES :] = got[: channels - full * LANES]


VM, HB = pltpu.VMEM, pltpu.HBM


def call(kernel, name, ins, outs, scratch=(), copies=0, flops=0, nbytes=0, mib=60):
    sems = [pltpu.SemaphoreType.DMA((copies,))] if copies else []
    return pl.pallas_call(
        kernel,
        name=name,
        out_shape=[jax.ShapeDtypeStruct(s, d) for s, d, _ in outs],
        in_specs=[pl.BlockSpec(memory_space=m) for m in ins],
        out_specs=[pl.BlockSpec(memory_space=m) for _, _, m in outs],
        scratch_shapes=[pltpu.VMEM(s, d) for s, d in scratch] + sems,
        compiler_params=params(mib),
        cost_estimate=pl.CostEstimate(flops=flops, bytes_accessed=nbytes, transcendentals=0) if nbytes else None,
    )


def pack(f):
    channels, nrows, lons = f.shape
    wide = -(-channels // LANES) * LANES
    edge = ((16, wide), BF16, VM)
    return call(
        pack_kernel, "pack", [VM], [((nrows, lons, wide), BF16, VM), edge, edge],
        [((nrows * wide, lons), F32)], mib=16,
    )(f)


def padded_shape(ft):
    nrows, lons, wide = ft.shape
    return wide // LANES, nrows, lons + 2 * PAD, LANES


def forward(members, ft, hl, hr, wt, up, down, head):
    nrows, lons, wide = ft.shape
    points = nrows * lons
    channels, hiddens = down.shape
    xhat, inv, pre = ((wide // LANES, nrows, lons, LANES), F32), ((nrows, lons, 1), F32), ((points, hiddens), F32)
    return call(
        functools.partial(forward_kernel, channels), "forward", [HB] * 7,
        [((members, head.shape[0] * nrows // members, lons), BF16, VM), (*xhat, HB), (*inv, HB), (*pre, HB)],
        [(padded_shape(ft), F32), ((points, wide), BF16), ((points, hiddens), BF16), xhat, inv, pre,
         (up.shape, BF16), (down.shape, BF16), (head.shape, BF16)]
        + [(v.shape, v.dtype) for v in (ft, hl, hr, wt)], 10,
    )(ft, hl, hr, wt, up, down, head)


def gelu_slope(pre):
    points, hiddens = pre.shape
    tall = points // 8
    return pl.pallas_call(
        slope_kernel,
        name="slope",
        grid=(8,),
        out_shape=jax.ShapeDtypeStruct(pre.shape, BF16),
        in_specs=[pl.BlockSpec((tall, hiddens), lambda i: (i, 0))],
        out_specs=pl.BlockSpec((tall, hiddens), lambda i: (i, 0)),
        compiler_params=params(),
        cost_estimate=pl.CostEstimate(flops=20 * pre.size, bytes_accessed=8 * pre.size, transcendentals=0),
    )(pre)


def backward(members, pieces, right, pred, obs, pair, hl, hr, wt, up, down, head, xhat, inv, gslope, ft):
    tiles, nrows, lons, _ = xhat.shape
    points, wide = nrows * lons, tiles * LANES
    channels, hiddens = down.shape
    sums = pieces * (4 if 4 * pieces >= 56 else 16)
    tall = 3 * nrows + sums // pieces
    direct = ((tiles, points, LANES), BF16)
    far = (pred, obs, pair, hl, hr, wt, up, down, head, xhat, inv, gslope, ft)
    return call(
        functools.partial(backward_kernel, channels, members), "backward", [pltpu.SMEM] + [HB] * 13,
        [(obs.shape, F32, VM), (xhat.shape, F32, HB), (*direct, HB), ((pieces, tall, wide), BF16, VM)],
        [((points, hiddens), BF16), (xhat.shape, F32), direct, ((tiles, sums, LANES), F32), (padded_shape(ft), F32)]
        + [(v.shape, v.dtype) for v in far],
        15, 224 * xhat.size, 8 * xhat.size,
    )(right, *far)


def pairs(p):
    members, _, lanes = p.shape
    return call(
        pair_kernel, "pairs", [VM], [(p.shape, BF16, VM)],
        [(p.shape, F32), ((2 * members, lanes), F32), ((2, 2 * members, lanes), F32), (p.shape, F32)], mib=16,
    )(p)[0]


def adjoint(channels, cot, hl, hr, wt, direct):
    tiles, nrows, lons, _ = cot.shape
    tall = LANES * nrows
    return call(
        adjoint_kernel, "adjoint", [HB, VM, VM, VM, HB], [((channels, nrows, lons), BF16, VM)],
        [((tiles, nrows, lons + 2 * PAD, LANES), F32), ((tall, tall), BF16), ((lons, tall), BF16), (direct.shape, BF16)],
        2, 224 * cot.size, 8 * cot.size,
    )(cot, hl, hr, wt, direct)[0]


def ring(axis):
    n = lax.axis_size(axis)
    up = [(i, (i + 1) % n) for i in range(n)]
    return up, [(j, i) for i, j in up]


def swap_edges(to_right, to_left):
    up, down = ring("lon")
    return lax.ppermute(to_right, "lon", up), lax.ppermute(to_left, "lon", down)


def shards(fields, observed, conv_weight, norm_gain, up_weight, down_weight, head_weight):
    _, channels, nrows, lons = fields.shape
    nvars = observed.shape[0]
    members, pieces = lax.axis_size("ens"), lax.axis_size("lon")
    up_weight = up_weight.T
    ft, to_right, to_left = pack(fields[0])
    hl, hr = swap_edges(to_right, to_left)
    tiles = ft.shape[2] // LANES
    wt = jnp.concatenate([conv_weight.T, norm_gain[None]], 0)
    wt = jnp.pad(wt, ((0, 6), (0, tiles * LANES - channels))).reshape(56, tiles, LANES).transpose(1, 0, 2)
    pred, xhat, inv, pre = forward(members, ft, hl, hr, wt, up_weight, down_weight, head_weight)
    met = exchange(pred, "ens")
    pair = exchange(pairs(met), "ens")
    gslope = gelu_slope(pre)
    here = lax.axis_index("lon")
    before, after = (here + pieces - 1) % pieces, (here + 1) % pieces
    score, cot, direct, sent = backward(
        members, pieces, after[None], pred, observed.reshape(nvars, -1), pair, hl, hr, wt,
        up_weight, down_weight, head_weight, xhat, inv, gslope, ft,
    )
    met = exchange(sent, "lon")
    field_out, total = reduce_beside(
        jnp.sum(met[:, 3 * nrows :].astype(F32), 0).astype(BF16),
        lambda: adjoint(channels, cot, met[before], met[after], wt, direct),
    )
    return (field_out[None], score.reshape(1, nvars, nrows, lons), total[:49, :channels].T, total[49, :channels])


def exchange(x, axis):
    return lax.all_to_all(x, axis, 0, 0, tiled=True)


def reduce_beside(mine, work):
    deep, wide = mine.shape
    pieces = lax.axis_size("lon")
    parts = exchange(jnp.broadcast_to(mine, (lax.axis_size("ens"), deep, wide)), "ens")
    parts, done = lax.optimization_barrier((parts, work()))
    mine = jnp.sum(parts.astype(F32), 0).astype(BF16)
    total = exchange(jnp.broadcast_to(mine, (pieces, deep, wide)), "lon").astype(F32)
    return done, total.reshape(pieces * deep, wide)


def solution(mesh):
    in_specs = (P("ens", None, None, "lon"), P(None, None, "lon"), P(), P(), P(), P(), P())
    out_specs = (P("ens", None, None, "lon"), P("ens", None, None, "lon"), P(), P())
    return jax.shard_map(shards, mesh=mesh, in_specs=in_specs, out_specs=out_specs, check_vma=False)
```
